32 devices in a mesh: dp: 8 (over y, x, core), mp: 4 (over z).
Axes of the slice: x: 2, y: 2, z: 4, core: 2. Of those that a mesh axis runs over, the one named last changes fastest.
Arguments:
- buffer: bfloat16 [65536, 256], P(('dp', 'mp')), may hold values from -24 to 24, as said below
- owner: int32 [32768, 1], P(('dp', 'mp')), may hold values from 0 to 31; in each aligned block of 1024 rows (0 to 1023, 1024 to 2047, ...) at most 128 rows name the same one
- local_row: int32 [32768], P(('dp', 'mp')), may hold values from 0 to 2047
- q_in: bfloat16 [2, 130, 256], replicated, may hold values from -0.5 to 0.5
- q_mid: bfloat16 [2, 256, 256], replicated, may hold values from -0.5 to 0.5
- q_out: bfloat16 [2, 256], replicated, may hold values from -0.5 to 0.5
- v_in: bfloat16 [124, 256], replicated, may hold values from -0.5 to 0.5
- v_mid: bfloat16 [256, 256], replicated, may hold values from -0.5 to 0.5
- v_out: bfloat16 [256], replicated, may hold values from -0.5 to 0.5
Outputs:
- q_values: float32 [2, 32768], P(None, ('dp', 'mp'))
- values: float32 [2, 32768], P(None, ('dp', 'mp'))
- targets: float32 [32768], P(('dp', 'mp'))
- q_loss: float32 [32768], P(('dp', 'mp'))
- value_loss: float32 [32768], P(('dp', 'mp'))
The draws below stay inside these ranges and needn't reach their ends.
Inputs may be any that keep to these rules, and one draw needn't show every extreme that they name: Owner o is the replay owner at position o of the devices in dp+mp order. In the rows of one reader no owner is named more than 128 times, a bound that some block reaches. `buffer`: action values lie in -1 to 1 and discounts in 0 to 0.99.
All inputs are finite; a program needn't handle non-finite values.
Results may differ from the reference program's by a relative error of at most 0.005.
Values may be sent and summed in bfloat16 or wider, within the bound.
A program may use at most 64 MiB of HBM per device.

```python
import math
import jax
import jax.numpy as jnp
import numpy as np
from jax import lax

S = 124
A = 6
H = 256
ROWS_DEV = 2048
B_DEV = 1024
CAP = 128
ROWS = 65536
BATCH = 32768
DEVICES = 32


def draw_buffer(key, part):
    keys = jax.random.split(jax.random.fold_in(key, 17), 5)
    states = jnp.clip(jax.random.normal(keys[0], (ROWS, S), jnp.float32), -6.0, 6.0)
    actions = jax.random.uniform(keys[1], (ROWS, A), jnp.float32, -1.0, 1.0)
    nexts = jnp.clip(jax.random.normal(keys[2], (ROWS, S), jnp.float32), -6.0, 6.0)
    reward = jnp.clip(jax.random.normal(keys[3], (ROWS, 1), jnp.float32), -6.0, 6.0)
    discount = jax.random.uniform(keys[4], (ROWS, 1), jnp.float32, 0.0, 0.99)
    return jnp.concatenate([states, actions, nexts, reward, discount], axis=1).astype(jnp.bfloat16)


def with_ends(result, key, low, largest):
    dims = result.shape
    place = [jax.random.randint(jax.random.fold_in(key, axis), (), 0, dims[axis]) for axis in range(len(dims))]
    result = result.at[tuple(place)].set(low)
    longest = dims.index(max(dims))
    place[longest] = (place[longest] + 1) % dims[longest]
    return result.at[tuple(place)].set(largest)


def assign_block(stream_key, own, number, rows, count, top, bound, skew):
    order = jax.random.permutation(stream_key, count)
    heavy_load, common = shares(count, rows * top, bound, skew, True), shares(count, rows * top, bound, skew, False)
    places = jnp.arange(count)

    def named(sizes, rotation):
        used = int((sizes > 0).sum())
        fixed = max(1, used // 4)
        moved = fixed + (places - fixed + rotation * (used - fixed)) % max(1, count - fixed)
        return jnp.zeros((count,), jnp.int32).at[order[jnp.where(places < fixed, places, moved)]].set(jnp.asarray(sizes, jnp.int32))

    sizes = jnp.where(number % 4 == 0, named(heavy_load, number // 4), named(common, number - number // 4 - 1))
    mixed = jax.random.permutation(jax.random.fold_in(own, 3), count)
    donor, taker = mixed[0:count // 2 * 2:2], mixed[1:count // 2 * 2:2]
    room = jnp.minimum(sizes[donor] - 1, bound - sizes[taker]) // 2
    room = jnp.where((donor == order[0]) | (taker == order[0]) | (sizes[taker] == 0), 0, jnp.maximum(room, 0))
    moved = jax.random.randint(jax.random.fold_in(own, 4), (count // 2,), 0, 1 << 20) % (room + 1)
    sizes = sizes.at[donor].add(-moved).at[taker].add(moved)
    members = jnp.searchsorted(jnp.cumsum(sizes), jnp.arange(rows * top), side="right").astype(jnp.int32)
    listing = members.reshape(top, rows).T
    listing = listing[jax.random.permutation(jax.random.fold_in(own, 1), rows)]
    rotation = jax.random.randint(jax.random.fold_in(own, 2), (rows, 1), 0, top)
    return jnp.take_along_axis(listing, (jnp.arange(top)[None, :] + rotation) % top, axis=1)


def shares(number_of, total, reach, skew, full):
    weights = [(1 << 20) // math.isqrt(grade ** skew) + 1 for grade in range(1, number_of + 1)]
    largest = reach if full else min(reach, max(-(-total // number_of), total * weights[0] // sum(weights)))
    least = 1 if total - largest >= number_of - 1 else 0
    holding, surplus = [largest] + [least] * (number_of - 1), total - largest - least * (number_of - 1)
    while surplus > 0:
        candidates = [i for i in range(1, number_of) if holding[i] < largest] or [i for i in range(1, number_of) if holding[i] < reach]
        whole, remaining = sum([weights[i] for i in candidates]), surplus
        for i in candidates:
            more = min(reach - holding[i], max(1, remaining * weights[i] // whole), surplus)
            holding[i] = holding[i] + more
            surplus = surplus - more
    return np.array(holding)


def scatter_about(key, extent, spread, bound, kind=jnp.bfloat16):
    drawn = spread * jax.random.normal(key, extent, jnp.float32)
    return jnp.clip(drawn, min=-bound, max=bound).astype(kind)


def setup_inputs(seed: int = 0) -> dict:
    splits = jax.random.split(jax.random.key(seed), 10)
    buffer = draw_buffer(jax.random.fold_in(splits[9], 71), 0)
    owner_keys = jax.random.split(jax.random.fold_in(splits[1], 1), BATCH // B_DEV)
    owner_turns = jax.random.permutation(jax.random.fold_in(splits[1], 3), BATCH // B_DEV)
    owner = jax.vmap(lambda own, number: assign_block(jax.random.fold_in(splits[1], 2), own, number, B_DEV, DEVICES, 1, CAP, 2))(owner_keys, owner_turns).reshape((BATCH, 1))
    local_row = with_ends(jax.random.randint(splits[2], (BATCH,), 0, ROWS_DEV), jax.random.fold_in(splits[2], 1), 0, ROWS_DEV - 1).astype(jnp.int32)
    q_in = scatter_about(splits[3], (2, S + A, H), (S + A) ** -0.5, 0.5)
    q_mid = scatter_about(splits[4], (2, H, H), (H // 2) ** -0.5, 0.5)
    q_out = scatter_about(splits[5], (2, H), (H // 2) ** -0.5, 0.5)
    v_in = scatter_about(splits[6], (S, H), S ** -0.5, 0.5)
    v_mid = scatter_about(splits[7], (H, H), (H // 2) ** -0.5, 0.5)
    v_out = scatter_about(splits[8], (H,), (H // 2) ** -0.5, 0.5)
    return dict(buffer=buffer, owner=owner, local_row=local_row, q_in=q_in, q_mid=q_mid, q_out=q_out, v_in=v_in, v_mid=v_mid, v_out=v_out)


def layer_two(first, mid, out):
    hidden = jnp.maximum(jnp.dot(first, mid, preferred_element_type=jnp.float32), 0.0)
    return jnp.dot(hidden, out.astype(jnp.float32), precision=lax.Precision.HIGHEST)


def critic_block(rows, q_in, q_mid, q_out, v_in, v_mid, v_out):
    pair = rows[:, :S + A]
    state = rows[:, :S]
    nexts = rows[:, S + A:2 * S + A]
    reward = rows[:, 2 * S + A].astype(jnp.float32)
    discount = rows[:, 2 * S + A + 1].astype(jnp.float32)
    qs = []
    for head in range(2):
        first = jnp.maximum(jnp.dot(pair, q_in[head], preferred_element_type=jnp.float32), 0.0).astype(jnp.bfloat16)
        qs.append(layer_two(first, q_mid[head], q_out[head]))
    both = jnp.concatenate([state, nexts], axis=0)
    vfirst = jnp.maximum(jnp.dot(both, v_in, preferred_element_type=jnp.float32), 0.0).astype(jnp.bfloat16)
    vall = layer_two(vfirst, v_mid, v_out)
    batch = state.shape[0]
    value_now = vall[:batch]
    value_next = vall[batch:]
    targets = reward + discount * value_next
    return qs[0], qs[1], value_now, value_next, targets


def reference(buffer, owner, local_row, q_in, q_mid, q_out, v_in, v_mid, v_out):
    index = (owner[:, 0] * ROWS_DEV + local_row).astype(jnp.int32)
    blocks = index.reshape(-1, B_DEV)

    def one_block(picks):
        rows = jnp.take(buffer, picks, axis=0)
        return critic_block(rows, q_in, q_mid, q_out, v_in, v_mid, v_out)

    results = lax.map(one_block, blocks)
    q_first, q_second, value_now, value_next, targets = [r.reshape(-1) for r in results]
    q_loss = (q_first - targets) ** 2 + (q_second - targets) ** 2
    gap = jnp.minimum(q_first, q_second) - value_now
    value_loss = jnp.where(gap < 0.0, 0.3, 0.7) * gap * gap
    return jnp.stack([q_first, q_second]), jnp.stack([value_now, value_next]), targets, q_loss, value_loss
```

```python
import functools

import jax
import jax.numpy as jnp
from jax import lax
from jax.experimental import pallas as pl
from jax.experimental.pallas import tpu as pltpu
from jax.sharding import PartitionSpec as P

MESH = pl.DeviceIdType.MESH
KINDS = 5
CHUNKS = 4
UNROLL = 64
f32, bf16, i32 = jnp.float32, jnp.bfloat16, jnp.int32


def iota(shape, axis):
    return lax.broadcasted_iota(i32, shape, axis)


def split(value):
    high = value.astype(bf16)
    return high, (value - high.astype(f32)).astype(bf16)


def kernel(
    dp_size,
    mp_size,
    slots,
    buffer,
    owner_hbm,
    row_hbm,
    q_in_hbm,
    q_mid_hbm,
    q_out_hbm,
    v_in_hbm,
    v_mid_hbm,
    v_out_hbm,
    result_ref,
    owner_ref,
    row_ref,
    q_in_ref,
    q_mid_ref,
    q_out_ref,
    v_in_ref,
    v_mid_ref,
    v_out_ref,
    rows_v,
    first_w,
    h1_ref,
    table,
    halves,
    hot,
    ask_out,
    ask_in,
    reply_out,
    reply_in,
    load_sem,
    fetch_sem,
    ask_send,
    ask_recv,
    reply_send,
    reply_recv,
):
    owners = dp_size * mp_size
    pairs = owners // 2
    rows_dev, width = buffer.shape
    hidden = v_mid_ref.shape[0]
    states = v_in_ref.shape[0]
    inputs = q_in_ref.shape[0]
    batch = row_ref.shape[1]
    columns = rows_dev // 8
    dp, mp = lax.axis_index("dp"), lax.axis_index("mp")
    me = dp * mp_size + mp

    fetches = [
        pltpu.make_async_copy(source, target, fetch_sem.at[number])
        for number, (source, target) in enumerate(
            (
                (owner_hbm, owner_ref),
                (row_hbm, row_ref),
                (q_in_hbm, q_in_ref),
                (v_in_hbm, v_in_ref),
                (q_mid_hbm, q_mid_ref),
                (v_mid_hbm, v_mid_ref),
                (q_out_hbm, q_out_ref),
                (v_out_hbm, v_out_ref),
            )
        )
    ]
    for fetch in fetches:
        fetch.start()
    part = rows_dev // CHUNKS
    loads = [
        pltpu.make_async_copy(
            buffer.at[pl.ds(n * part, part)], rows_v.at[pl.ds(n * part, part)], load_sem.at[n]
        )
        for n in range(CHUNKS)
    ]
    for load in loads:
        load.start()

    def partner(k):
        there = [mp, dp]
        for bit in range(k.bit_length()):
            if (k >> bit) & 1:
                axis, step = (0, 1 << bit) if (1 << bit) < mp_size else (1, (1 << bit) // mp_size)
                there[axis] = there[axis] + step * (1 - 2 * ((there[axis] // step) % 2))
        return (there[1], there[0])

    far = list(range(owners - 1, 0, -1))
    reply_in[...] = jnp.zeros_like(reply_in)
    barrier = pltpu.get_barrier_semaphore()
    for k in far:
        pl.semaphore_signal(barrier, inc=1, device_id=partner(k), device_id_type=MESH)

    def ask(k):
        here = (k % 2, pl.ds(k // 2, 1))
        return pltpu.make_async_remote_copy(
            src_ref=ask_out.at[here],
            dst_ref=ask_in.at[here],
            send_sem=ask_send.at[k],
            recv_sem=ask_recv.at[k],
            device_id=partner(k),
            device_id_type=MESH,
        )

    def reply(k):
        here = (k, pl.ds(0, KINDS))
        return pltpu.make_async_remote_copy(
            src_ref=reply_out.at[here],
            dst_ref=reply_in.at[here],
            send_sem=reply_send.at[k],
            recv_sem=reply_recv.at[k],
            device_id=partner(k),
            device_id_type=MESH,
        )

    for fetch in fetches[:2]:
        fetch.wait()
    relative = owner_ref[...] ^ me
    pair_of = relative // 2
    row = row_ref[...]
    span = 256
    named = jnp.where(iota((owners, batch), 0) == relative, 1.0, 0.0)
    before = jnp.where(iota((span, span), 0) < iota((span, span), 1), 1.0, 0.0).astype(bf16)
    counts = jnp.dot(
        jnp.concatenate([named[:, n : n + span] for n in range(0, batch, span)], axis=0).astype(bf16),
        before,
        preferred_element_type=f32,
    )
    offset = jnp.zeros((owners, 1), f32)
    ranks = []
    for n in range(batch // span):
        mine = named[:, n * span : (n + 1) * span]
        count = counts[n * owners : (n + 1) * owners]
        ranks.append(jnp.sum(mine * (count + offset), axis=0, keepdims=True))
        offset = offset + count[:, span - 1 : span] + mine[:, span - 1 : span]
    rank = jnp.concatenate(ranks, axis=1).astype(i32)
    place = rank + (relative & 1) * slots
    hot[...] = jnp.where(iota((2 * slots, batch), 0) == place, 1.0, 0.0).astype(bf16)
    listed = iota((pairs, batch), 0) == pair_of
    wanted = jnp.concatenate(
        [
            jnp.where(listed, (row // 8).astype(f32), 0.0),
            jnp.where(listed, (row & 7).astype(f32), 0.0),
        ],
        axis=0,
    ).astype(bf16)
    found = lax.dot_general(
        wanted, hot[...], (((1,), (1,)), ((), ())), preferred_element_type=f32
    )
    asked = (found[:pairs] * 8.0 + found[pairs:]).astype(i32)
    for side in range(2):
        ask_out[side] = asked[:, side * slots : (side + 1) * slots]
    ask_in[0, 0:1] = asked[0:1, 0:slots]

    for fetch in fetches[2:]:
        fetch.wait()
    first_w[...] = jnp.zeros_like(first_w)
    for head in range(2):
        first_w[0:inputs, head * hidden : (head + 1) * hidden] = q_in_ref[:, head, :]
    first_w[0:states, 2 * hidden : 3 * hidden] = v_in_ref[...]
    first_w[inputs : inputs + states, 3 * hidden : 4 * hidden] = v_in_ref[...]
    outs = [q_out_ref[n : n + 1, :].astype(f32) for n in range(2)]
    outs.append(v_out_ref[...].astype(f32).reshape(1, hidden))

    lane = iota((8, 128), 1)
    tiles = columns // 128
    sums = [[jnp.zeros((8, 128), f32) for _ in range(tiles)] for _ in range(6)]

    def collect(kind, first, column):
        for n in range(column.shape[0] // 8):
            tile, at = divmod(first // 8 + n, 128)
            value = jnp.broadcast_to(column[n * 8 : (n + 1) * 8], (8, 128))
            sums[kind][tile] = jnp.where(lane == at, value, sums[kind][tile])

    for n in range(CHUNKS):
        loads[n].wait()
        block = rows_v[n * part : (n + 1) * part, :]
        for head in range(4):
            own = slice(head * hidden, (head + 1) * hidden)
            h1 = jnp.dot(block, first_w[:, own], preferred_element_type=f32)
            h1_ref[:, own] = jnp.maximum(h1, 0.0).astype(bf16)
        for head in range(4):
            own = slice(head * hidden, (head + 1) * hidden)
            second_w = q_mid_ref[head] if head < 2 else v_mid_ref[...]
            h2 = jnp.dot(h1_ref[:, own], second_w, preferred_element_type=f32)
            terms = jnp.maximum(h2, 0.0) * outs[min(head, 2)]
            terms = sum(terms[:, m : m + 128] for m in range(0, hidden, 128))
            collect(head, n * part, jnp.sum(terms, axis=1, keepdims=True))
        tail = block[:, width - 128 :].astype(f32)
        ends = inputs + states - (width - 128)
        for m in range(2):
            collect(4 + m, n * part, tail[:, ends + m : ends + m + 1])

    pl.semaphore_wait(barrier, owners - 1)
    for k in far:
        ask(k).start()

    table[...] = jnp.zeros_like(table)
    for tile in range(tiles):
        *values, reward, discount = [kind[tile] for kind in sums]
        values.append(reward + discount * values[3])
        for kind, value in enumerate(values):
            table[tile, pl.ds(kind, 8, stride=8), :] = value
    for tile in range(tiles):
        halves[:, tile * 128 : (tile + 1) * 128] = jnp.concatenate(split(table[tile]), axis=0)

    def answer(pair):
        code = jnp.concatenate(
            [ask_in[side, pl.ds(pair, 1), :] for side in range(2)], axis=1
        )
        pick = jnp.where(iota((columns, 2 * slots), 0) == code // 8, 1.0, 0.0).astype(bf16)
        both = jnp.dot(halves[...], pick, preferred_element_type=f32)
        both = both[:64] + both[64:]
        low = jnp.broadcast_to(code & 7, (8, 2 * slots))
        value = both[0:8]
        for n in range(1, 8):
            value = jnp.where(low == n, both[n * 8 : (n + 1) * 8], value)
        return [value[:, side * slots : (side + 1) * slots] for side in range(2)]

    if owners <= UNROLL:
        for pair in reversed(range(pairs)):
            for side in range(2):
                if pair + side:
                    ask(2 * pair + side).wait_recv()
            for side, value in enumerate(answer(pair)):
                k = 2 * pair + side
                if k:
                    reply_out[k] = value
                    reply(k).start()
                else:
                    reply_in[k] = value
    else:
        for k in far:
            ask(k).wait_recv()

        def step(n, carry):
            for side, value in enumerate(answer(n)):
                reply_out[2 * n + side] = value
            return carry

        lax.fori_loop(0, pairs, step, 0)
        for k in far:
            reply(k).start()
        reply_in[0] = reply_out[0]

    for k in far:
        ask(k).wait_send()

    where = jnp.broadcast_to(pair_of, (8, batch))
    acc = jnp.zeros((8, batch), f32)
    some = 4

    def gather(acc, start):
        sources = [
            jnp.concatenate([reply_in[2 * (start + n)], reply_in[2 * (start + n) + 1]], axis=1)
            for n in range(some)
        ]
        high, low = split(jnp.concatenate(sources, axis=0))
        both = jnp.dot(
            jnp.concatenate([high, low], axis=0), hot[...], preferred_element_type=f32
        )
        both = both[: some * 8] + both[some * 8 :]
        for n in range(some):
            acc = jnp.where(where == start + n, both[n * 8 : (n + 1) * 8], acc)
        return acc

    if owners <= UNROLL:
        for start in range(0, pairs, some):
            if start + some == pairs:
                for k in far:
                    reply(k).wait_send()
            for k in range(max(1, 2 * start), 2 * (start + some)):
                reply(k).wait_recv()
            acc = gather(acc, start)
    else:
        for k in far:
            reply(k).wait()
        acc = lax.fori_loop(0, pairs // some, lambda n, a: gather(a, n * some), acc)
    result_ref[...] = acc


def spread(result_ref, q_values_ref, values_ref, targets_ref, q_loss_ref, value_loss_ref):
    q_first, q_second = result_ref[0:1], result_ref[1:2]
    targets = result_ref[4:5]
    q_values_ref[...] = result_ref[0:2]
    values_ref[...] = result_ref[2:4]
    targets_ref[...] = targets
    q_loss_ref[...] = (q_first - targets) ** 2 + (q_second - targets) ** 2
    gap = jnp.minimum(q_first, q_second) - result_ref[2:3]
    value_loss_ref[...] = jnp.where(gap < 0.0, 0.3, 0.7) * gap * gap


def body(buffer, owner, local_row, q_in, q_mid, q_out, v_in, v_mid, v_out):
    dp_size, mp_size = lax.axis_size("dp"), lax.axis_size("mp")
    owners = dp_size * mp_size
    batch = local_row.shape[0]
    rows_dev, width = buffer.shape
    hidden = v_mid.shape[0]
    most = 4 * batch // owners
    slots = -(-most // 128) * 128
    vmem = pl.BlockSpec(memory_space=pltpu.VMEM)
    hbm = pl.BlockSpec(memory_space=pltpu.HBM)
    dma = pltpu.SemaphoreType.DMA
    result = pl.pallas_call(
        functools.partial(kernel, dp_size, mp_size, slots),
        out_shape=pltpu.VMEM((8, batch), f32),
        in_specs=[hbm] * 9,
        out_specs=vmem,
        scratch_shapes=[
            pltpu.VMEM((1, batch), i32),
            pltpu.VMEM((1, batch), i32),
            pltpu.VMEM((q_in.shape[1], 2, hidden), bf16),
            pltpu.VMEM(q_mid.shape, bf16),
            pltpu.VMEM(q_out.shape, bf16),
            pltpu.VMEM(v_in.shape, bf16),
            pltpu.VMEM(v_mid.shape, bf16),
            pltpu.VMEM(v_out.shape, bf16),
            pltpu.VMEM((rows_dev, width), bf16),
            pltpu.VMEM((width, 4 * hidden), bf16),
            pltpu.VMEM((rows_dev // CHUNKS, 4 * hidden), bf16),
            pltpu.VMEM((rows_dev // 8 // 128, 64, 128), f32),
            pltpu.VMEM((128, rows_dev // 8), bf16),
            pltpu.VMEM((2 * slots, batch), bf16),
            pltpu.VMEM((2, owners // 2, slots), i32),
            pltpu.VMEM((2, owners // 2, slots), i32),
            pltpu.VMEM((owners, 8, slots), f32),
            pltpu.VMEM((owners, 8, slots), f32),
            dma((CHUNKS,)),
            dma((8,)),
            dma((owners,)),
            dma((owners,)),
            dma((owners,)),
            dma((owners,)),
        ],
        compiler_params=pltpu.CompilerParams(
            collective_id=0, has_side_effects=True, vmem_limit_bytes=48 << 20
        ),
        name="critic_exchange",
    )(
        *(
            pltpu.with_memory_space_constraint(x, pltpu.HBM)
            for x in (
                buffer,
                owner.reshape(1, batch),
                local_row.reshape(1, batch),
                jnp.transpose(q_in, (1, 0, 2)),
                q_mid,
                q_out,
                v_in,
                v_mid,
                v_out,
            )
        )
    )
    one = jax.ShapeDtypeStruct((1, batch), f32)
    two = jax.ShapeDtypeStruct((2, batch), f32)
    outs = pl.pallas_call(
        spread,
        out_shape=(two, two, one, one, one),
        in_specs=[vmem],
        out_specs=(vmem,) * 5,
        compiler_params=pltpu.CompilerParams(vmem_limit_bytes=1 << 20),
        name="spread",
    )(result)
    q_values, values, targets, q_loss, value_loss = outs
    return (
        q_values,
        values,
        targets.reshape(batch),
        q_loss.reshape(batch),
        value_loss.reshape(batch),
    )


def solution(mesh):
    rows = P(("dp", "mp"))
    sides = P(None, ("dp", "mp"))
    return jax.shard_map(
        body,
        mesh=mesh,
        in_specs=(P(("dp", "mp"), None), P(("dp", "mp"), None), rows) + (P(),) * 6,
        out_specs=(sides, sides, rows, rows, rows),
        check_vma=False,
    )
```

```python
import functools

import jax
import jax.numpy as jnp
from jax import lax
from jax.experimental import pallas as pl
from jax.experimental.pallas import tpu as pltpu
from jax.sharding import PartitionSpec as P

MESH = pl.DeviceIdType.MESH
CHUNKS = 4
UNROLL = 64
f32, bf16, i32 = jnp.float32, jnp.bfloat16, jnp.int32


def iota(shape, axis):
    return lax.broadcasted_iota(i32, shape, axis)


def kernel(
    dp_size,
    mp_size,
    slots,
    buffer,
    owner_hbm,
    row_hbm,
    q_in_hbm,
    q_mid_hbm,
    q_out_hbm,
    v_in_hbm,
    v_mid_hbm,
    v_out_hbm,
    result_ref,
    owner_ref,
    row_ref,
    q_in_ref,
    q_mid_ref,
    q_out_ref,
    v_in_ref,
    v_mid_ref,
    v_out_ref,
    rows_v,
    first_w,
    h1_ref,
    draft,
    tables,
    hot,
    picks,
    ask_out,
    ask_in,
    reply_out,
    reply_in,
    load_sem,
    fetch_sem,
    push_send,
    push_recv,
    ask_send,
    ask_recv,
    reply_send,
    reply_recv,
):
    owners = dp_size * mp_size
    pairs = owners // 2
    halves = mp_size // 2
    rows_dev, width = buffer.shape
    hidden = v_mid_ref.shape[0]
    states = v_in_ref.shape[0]
    inputs = q_in_ref.shape[0]
    batch = row_ref.shape[1]
    columns = rows_dev // 8
    dp, mp = lax.axis_index("dp"), lax.axis_index("mp")
    me = dp * mp_size + mp

    load = pltpu.make_async_copy(buffer, rows_v, load_sem)
    fetches = [
        pltpu.make_async_copy(source, target, fetch_sem.at[number])
        for number, (source, target) in enumerate(
            (
                (q_in_hbm, q_in_ref),
                (v_in_hbm, v_in_ref),
                (q_mid_hbm, q_mid_ref),
                (v_mid_hbm, v_mid_ref),
                (q_out_hbm, q_out_ref),
                (v_out_hbm, v_out_ref),
                (owner_hbm, owner_ref),
                (row_hbm, row_ref),
            )
        )
    ]
    fetches[0].start()
    fetches[1].start()
    load.start()
    for fetch in fetches[2:]:
        fetch.start()

    def flip(value, bits):
        for bit in range(bits.bit_length()):
            if (bits >> bit) & 1:
                step = 1 << bit
                value = value + step * (1 - 2 * ((value // step) % 2))
        return value

    def column_mate(k):
        return (dp, flip(mp, k))

    def plane_mate(q):
        return (flip(dp, q), mp)

    column_mates = range(mp_size - 1, 0, -1)
    plane_mates = range(dp_size - 1, 0, -1)
    barrier = pltpu.get_barrier_semaphore()
    for k in column_mates:
        pl.semaphore_signal(barrier, inc=1, device_id=column_mate(k), device_id_type=MESH)
    for q in plane_mates:
        pl.semaphore_signal(barrier, inc=1, device_id=plane_mate(q), device_id_type=MESH)

    def push(k):
        return pltpu.make_async_remote_copy(
            src_ref=tables.at[0],
            dst_ref=tables.at[k],
            send_sem=push_send.at[k],
            recv_sem=push_recv.at[k],
            device_id=column_mate(k),
            device_id_type=MESH,
        )

    def ask(q):
        return pltpu.make_async_remote_copy(
            src_ref=ask_out.at[q],
            dst_ref=ask_in.at[q],
            send_sem=ask_send.at[q],
            recv_sem=ask_recv.at[q],
            device_id=plane_mate(q),
            device_id_type=MESH,
        )

    def reply(q, half):
        return pltpu.make_async_remote_copy(
            src_ref=reply_out.at[q, half],
            dst_ref=reply_in.at[q, half],
            send_sem=reply_send.at[q, half],
            recv_sem=reply_recv.at[q, half],
            device_id=plane_mate(q),
            device_id_type=MESH,
        )

    for fetch in fetches:
        fetch.wait()
    first_w[...] = jnp.zeros_like(first_w)
    for head in range(2):
        first_w[0:inputs, head * hidden : (head + 1) * hidden] = q_in_ref[:, head, :]
    first_w[0:states, 2 * hidden : 3 * hidden] = v_in_ref[...]
    first_w[inputs : inputs + states, 3 * hidden : 4 * hidden] = v_in_ref[...]
    outs = [q_out_ref[n : n + 1, :].astype(f32) for n in range(2)]
    outs.append(v_out_ref[...].astype(f32).reshape(1, hidden))

    lane = iota((8, 128), 1)
    tiles = columns // 128
    part = rows_dev // CHUNKS
    sums = [[jnp.zeros((8, 128), f32) for _ in range(tiles)] for _ in range(6)]

    def collect(kind, first, column):
        for n in range(column.shape[0] // 8):
            tile, at = divmod(first // 8 + n, 128)
            value = jnp.broadcast_to(column[n * 8 : (n + 1) * 8], (8, 128))
            sums[kind][tile] = jnp.where(lane == at, value, sums[kind][tile])

    load.wait()
    for n in range(CHUNKS):
        block = rows_v[n * part : (n + 1) * part, :]
        for head in range(4):
            own = slice(head * hidden, (head + 1) * hidden)
            h1 = jnp.dot(block, first_w[:, own], preferred_element_type=f32)
            h1_ref[n, :, own] = jnp.maximum(h1, 0.0).astype(bf16)
        for head in range(4):
            own = slice(head * hidden, (head + 1) * hidden)
            second_w = q_mid_ref[head] if head < 2 else v_mid_ref[...]
            h2 = jnp.dot(h1_ref[n, :, own], second_w, preferred_element_type=f32)
            terms = jnp.maximum(h2, 0.0) * outs[min(head, 2)]
            terms = sum(terms[:, m : m + 128] for m in range(0, hidden, 128))
            collect(head, n * part, jnp.sum(terms, axis=1, keepdims=True))
        tail = block[:, width - 128 :].astype(f32)
        ends = inputs + states - (width - 128)
        for m in range(2):
            collect(4 + m, n * part, tail[:, ends + m : ends + m + 1])

    for tile in range(tiles):
        q_first, q_second, value_now, value_next, reward, discount = [
            kind[tile] for kind in sums
        ]
        targets = reward + discount * value_next
        q_loss = (q_first - targets) ** 2 + (q_second - targets) ** 2
        gap = jnp.minimum(q_first, q_second) - value_now
        value_loss = jnp.where(gap < 0.0, 0.3, 0.7) * gap * gap
        kinds = (q_first, q_second, value_now, value_next, targets, q_loss, value_loss)
        for kind, value in enumerate(kinds + (jnp.zeros_like(q_loss),)):
            draft[tile, pl.ds(kind, 8, stride=8), :] = value
        tables[0, :, tile * 128 : (tile + 1) * 128] = draft[tile].astype(bf16)

    pl.semaphore_wait(barrier, dp_size + mp_size - 2)
    for k in column_mates:
        push(k).start()

    relative = owner_ref[...] ^ me
    plane = relative // mp_size
    row = row_ref[...]
    span = 256
    named = jnp.where(iota((owners, batch), 0) == relative, 1.0, 0.0)
    before = jnp.where(iota((span, span), 0) < iota((span, span), 1), 1.0, 0.0).astype(bf16)
    counts = jnp.dot(
        jnp.concatenate([named[:, n : n + span] for n in range(0, batch, span)], axis=0).astype(bf16),
        before,
        preferred_element_type=f32,
    )
    offset = jnp.zeros((owners, 1), f32)
    ranks = []
    for n in range(batch // span):
        mine = named[:, n * span : (n + 1) * span]
        count = counts[n * owners : (n + 1) * owners]
        ranks.append(jnp.sum(mine * (count + offset), axis=0, keepdims=True))
        offset = offset + count[:, span - 1 : span] + mine[:, span - 1 : span]
    rank = jnp.concatenate(ranks, axis=1).astype(i32)
    place = rank + (plane & 1) * slots
    hot[...] = jnp.where(iota((2 * slots, batch), 0) == place, 1.0, 0.0).astype(bf16)
    group = (plane // 2) * mp_size + (relative & (mp_size - 1))
    listed = iota((pairs, batch), 0) == group
    wanted = jnp.concatenate(
        [
            jnp.where(listed, (row // 8).astype(f32), 0.0),
            jnp.where(listed, (row & 7).astype(f32), 0.0),
        ],
        axis=0,
    ).astype(bf16)
    found = lax.dot_general(
        wanted, hot[...], (((1,), (1,)), ((), ())), preferred_element_type=f32
    )
    asked = (found[:pairs] * 8.0 + found[pairs:]).astype(i32)
    for q in range(dp_size):
        ask_out[q] = asked[
            (q // 2) * mp_size : (q // 2 + 1) * mp_size, (q % 2) * slots : (q % 2 + 1) * slots
        ]
    ask_in[0] = ask_out[0]
    for q in plane_mates:
        ask(q).start()

    where = jnp.broadcast_to(group, (8, batch))
    acc = jnp.zeros((8, batch), f32)

    def pick_of(code):
        return jnp.where(iota((columns, code.shape[1]), 0) == code // 8, 1.0, 0.0).astype(bf16)

    def chosen(found, code):
        low = jnp.broadcast_to(code & 7, (8, code.shape[1]))
        value = found[0:8]
        for n in range(1, 8):
            value = jnp.where(low == n, found[n * 8 : (n + 1) * 8], value)
        return value

    def gather(acc, half):
        source = jnp.concatenate(
            [
                jnp.concatenate([reply_in[q, half], reply_in[q + 1, half]], axis=1)
                for q in range(0, dp_size, 2)
            ],
            axis=0,
        )
        found = jnp.dot(source, hot[...], preferred_element_type=f32)
        for n in range(dp_size):
            match = where == (n // 2) * mp_size + 2 * half + n % 2
            acc = jnp.where(match, found[n * 8 : (n + 1) * 8], acc)
        return acc

    for q in reversed(plane_mates):
        ask(q).wait_recv()
    if owners <= UNROLL:
        codes = [
            jnp.concatenate([ask_in[q, k : k + 1, :] for q in range(dp_size)], axis=1)
            for k in range(mp_size)
        ]
        for k in range(mp_size):
            picks[k] = pick_of(codes[k])
        for half in range(halves):
            values = []
            for k in (2 * half, 2 * half + 1):
                if k:
                    push(k).wait_recv()
                found = jnp.dot(tables[k], picks[k], preferred_element_type=f32)
                values.append(chosen(found, codes[k]))
            both = jnp.concatenate(values, axis=0).astype(bf16)
            for q in (*plane_mates, 0):
                target = reply_out if q else reply_in
                target[q, half] = both[:, q * slots : (q + 1) * slots]
                if q:
                    reply(q, half).start()
        for k in column_mates:
            push(k).wait_send()
        for q in plane_mates:
            ask(q).wait_send()
        for half in range(halves):
            if half == halves - 1:
                for q in plane_mates:
                    for n in range(halves):
                        reply(q, n).wait_send()
            for q in reversed(plane_mates):
                reply(q, half).wait_recv()
            acc = gather(acc, half)
    else:
        for k in column_mates:
            push(k).wait()
        for q in plane_mates:
            ask(q).wait_send()

        def answer(n, carry):
            q, half = n // halves, n % halves
            values = []
            for m in range(2):
                code = ask_in[q, pl.ds(2 * half + m, 1), :]
                found = jnp.dot(tables[2 * half + m], pick_of(code), preferred_element_type=f32)
                values.append(chosen(found, code))
            reply_out[q, half] = jnp.concatenate(values, axis=0).astype(bf16)
            return carry

        lax.fori_loop(0, dp_size * halves, answer, 0)
        for half in range(halves):
            reply_in[0, half] = reply_out[0, half]
            for q in plane_mates:
                reply(q, half).start()
        for half in range(halves):
            for q in plane_mates:
                reply(q, half).wait()
        acc = lax.fori_loop(0, halves, lambda n, a: gather(a, n), acc)
    result_ref[...] = acc


def spread(result_ref, q_values_ref, values_ref, targets_ref, q_loss_ref, value_loss_ref):
    q_values_ref[...] = result_ref[0:2]
    values_ref[...] = result_ref[2:4]
    targets_ref[...] = result_ref[4:5]
    q_loss_ref[...] = result_ref[5:6]
    value_loss_ref[...] = result_ref[6:7]


def body(buffer, owner, local_row, q_in, q_mid, q_out, v_in, v_mid, v_out):
    dp_size, mp_size = lax.axis_size("dp"), lax.axis_size("mp")
    owners = dp_size * mp_size
    batch = local_row.shape[0]
    rows_dev, width = buffer.shape
    hidden = v_mid.shape[0]
    most = 4 * batch // owners
    slots = -(-most // 128) * 128
    vmem = pl.BlockSpec(memory_space=pltpu.VMEM)
    hbm = pl.BlockSpec(memory_space=pltpu.HBM)
    dma = pltpu.SemaphoreType.DMA
    result = pl.pallas_call(
        functools.partial(kernel, dp_size, mp_size, slots),
        out_shape=pltpu.VMEM((8, batch), f32),
        in_specs=[hbm] * 9,
        out_specs=vmem,
        scratch_shapes=[
            pltpu.VMEM((1, batch), i32),
            pltpu.VMEM((1, batch), i32),
            pltpu.VMEM((q_in.shape[1], 2, hidden), bf16),
            pltpu.VMEM(q_mid.shape, bf16),
            pltpu.VMEM(q_out.shape, bf16),
            pltpu.VMEM(v_in.shape, bf16),
            pltpu.VMEM(v_mid.shape, bf16),
            pltpu.VMEM(v_out.shape, bf16),
            pltpu.VMEM((rows_dev, width), bf16),
            pltpu.VMEM((width, 4 * hidden), bf16),
            pltpu.VMEM((CHUNKS, rows_dev // CHUNKS, 4 * hidden), bf16),
            pltpu.VMEM((rows_dev // 8 // 128, 64, 128), f32),
            pltpu.VMEM((mp_size, 64, rows_dev // 8), bf16),
            pltpu.VMEM((2 * slots, batch), bf16),
            pltpu.VMEM((mp_size, rows_dev // 8, dp_size * slots), bf16)
            if owners <= UNROLL
            else pltpu.VMEM((8, 128), f32),
            pltpu.VMEM((dp_size, mp_size, slots), i32),
            pltpu.VMEM((dp_size, mp_size, slots), i32),
            pltpu.VMEM((dp_size, mp_size // 2, 16, slots), bf16),
            pltpu.VMEM((dp_size, mp_size // 2, 16, slots), bf16),
            dma,
            dma((8,)),
            dma((mp_size,)),
            dma((mp_size,)),
            dma((dp_size,)),
            dma((dp_size,)),
            dma((dp_size, mp_size // 2)),
            dma((dp_size, mp_size // 2)),
        ],
        compiler_params=pltpu.CompilerParams(
            collective_id=0, has_side_effects=True, vmem_limit_bytes=48 << 20
        ),
        name="critic_exchange",
    )(
        *(
            pltpu.with_memory_space_constraint(x, pltpu.HBM)
            for x in (
                buffer,
                owner.reshape(1, batch),
                local_row.reshape(1, batch),
                jnp.transpose(q_in, (1, 0, 2)),
                q_mid,
                q_out,
                v_in,
                v_mid,
                v_out,
            )
        )
    )
    one = jax.ShapeDtypeStruct((1, batch), f32)
    two = jax.ShapeDtypeStruct((2, batch), f32)
    outs = pl.pallas_call(
        spread,
        out_shape=(two, two, one, one, one),
        in_specs=[vmem],
        out_specs=(vmem,) * 5,
        compiler_params=pltpu.CompilerParams(vmem_limit_bytes=1 << 20),
        name="spread",
    )(result)
    q_values, values, targets, q_loss, value_loss = outs
    return (
        q_values,
        values,
        targets.reshape(batch),
        q_loss.reshape(batch),
        value_loss.reshape(batch),
    )


def solution(mesh):
    rows = P(("dp", "mp"))
    sides = P(None, ("dp", "mp"))
    return jax.shard_map(
        body,
        mesh=mesh,
        in_specs=(P(("dp", "mp"), None), P(("dp", "mp"), None), rows) + (P(),) * 6,
        out_specs=(sides, sides, rows, rows, rows),
        check_vma=False,
    )
```

```python
import functools

import jax
import jax.numpy as jnp
from jax import lax
from jax.experimental import pallas as pl
from jax.experimental.pallas import tpu as pltpu
from jax.sharding import PartitionSpec as P

MESH = pl.DeviceIdType.MESH
CHUNKS = 4
UNROLL = 64
f32, bf16, i32 = jnp.float32, jnp.bfloat16, jnp.int32


def iota(shape, axis):
    return lax.broadcasted_iota(i32, shape, axis)


def kernel(
    dp_size,
    mp_size,
    slots,
    buffer,
    owner_hbm,
    row_hbm,
    q_in_hbm,
    q_mid_hbm,
    q_out_hbm,
    v_in_hbm,
    v_mid_hbm,
    v_out_hbm,
    result_ref,
    owner_ref,
    row_ref,
    q_in_ref,
    q_mid_ref,
    q_out_ref,
    v_in_ref,
    v_mid_ref,
    v_out_ref,
    rows_v,
    first_w,
    h1_ref,
    draft,
    tables,
    hot,
    picks,
    ask_out,
    ask_in,
    reply_out,
    reply_in,
    sibling_asks,
    far_tables,
    far_out,
    load_sem,
    fetch_sem,
    push_send,
    push_recv,
    ask_send,
    ask_recv,
    reply_send,
    reply_recv,
    sibling_send,
    sibling_recv,
    far_push_send,
    far_push_recv,
    far_send,
    far_recv,
):
    owners = dp_size * mp_size
    pairs = owners // 2
    halves = mp_size // 2
    rows_dev, width = buffer.shape
    hidden = v_mid_ref.shape[0]
    states = v_in_ref.shape[0]
    inputs = q_in_ref.shape[0]
    batch = row_ref.shape[1]
    columns = rows_dev // 8
    dp, mp = lax.axis_index("dp"), lax.axis_index("mp")
    me = dp * mp_size + mp

    load = pltpu.make_async_copy(buffer, rows_v, load_sem)
    fetches = [
        pltpu.make_async_copy(source, target, fetch_sem.at[number])
        for number, (source, target) in enumerate(
            (
                (q_in_hbm, q_in_ref),
                (v_in_hbm, v_in_ref),
                (q_mid_hbm, q_mid_ref),
                (v_mid_hbm, v_mid_ref),
                (q_out_hbm, q_out_ref),
                (v_out_hbm, v_out_ref),
                (owner_hbm, owner_ref),
                (row_hbm, row_ref),
            )
        )
    ]
    fetches[0].start()
    fetches[1].start()
    load.start()
    for fetch in fetches[2:]:
        fetch.start()

    def flip(value, bits):
        for bit in range(bits.bit_length()):
            if (bits >> bit) & 1:
                step = 1 << bit
                value = value + step * (1 - 2 * ((value // step) % 2))
        return value

    def column_mate(k):
        return (dp, flip(mp, k))

    def plane_mate(q):
        return (flip(dp, q), mp)

    column_mates = range(mp_size - 1, 0, -1)
    plane_mates = range(dp_size - 1, 0, -1)
    express = owners <= UNROLL
    last = mp_size - 2
    early = (mp == 0) & (dp // 2 == 0)
    source = (mp >= last) & (dp // 2 > 0)
    away = [(q, n) for n in range(2) for q in range(2, dp_size, 2)]
    barrier = pltpu.get_barrier_semaphore()
    for k in column_mates:
        pl.semaphore_signal(barrier, inc=1, device_id=column_mate(k), device_id_type=MESH)
    for q in plane_mates:
        pl.semaphore_signal(barrier, inc=1, device_id=plane_mate(q), device_id_type=MESH)

    if express:

        @pl.when(early)
        def _():
            for q, n in away:
                pl.semaphore_signal(
                    barrier, inc=1, device_id=(dp + q, last + n), device_id_type=MESH
                )

    def ready():
        mates = dp_size + mp_size - 2
        if express:
            pl.when(source)(lambda: pl.semaphore_wait(barrier, mates + 1))
            pl.when(jnp.logical_not(source))(lambda: pl.semaphore_wait(barrier, mates))
        else:
            pl.semaphore_wait(barrier, mates)

    rows_half = 32
    parts = range(2)

    def far_push(n):
        rows = pl.ds(n * rows_half, rows_half)
        there = (dp // 2 - 1, mp - last)
        return pltpu.make_async_remote_copy(
            src_ref=tables.at[0, rows],
            dst_ref=far_tables.at[(*there, rows)],
            send_sem=far_push_send.at[n],
            recv_sem=far_push_recv.at[(*there, n)],
            device_id=(dp % 2, 0),
            device_id_type=MESH,
        )

    def far_pushed(q, n, m):
        rows = pl.ds(m * rows_half, rows_half)
        return pltpu.make_async_remote_copy(
            src_ref=tables.at[0, rows],
            dst_ref=far_tables.at[q // 2 - 1, n, rows],
            send_sem=far_push_send.at[m],
            recv_sem=far_push_recv.at[q // 2 - 1, n, m],
            device_id=(dp + q, last + n),
            device_id_type=MESH,
        )

    def sibling_ask():
        return pltpu.make_async_remote_copy(
            src_ref=ask_out,
            dst_ref=sibling_asks,
            send_sem=sibling_send,
            recv_sem=sibling_recv,
            device_id=plane_mate(1),
            device_id_type=MESH,
        )

    def far_reply(q):
        return pltpu.make_async_remote_copy(
            src_ref=far_out.at[q // 2 - 1],
            dst_ref=reply_in.at[q + 1, halves - 1],
            send_sem=far_send.at[q // 2 - 1],
            recv_sem=far_recv.at[q // 2 - 1],
            device_id=plane_mate(1),
            device_id_type=MESH,
        )

    def push(k, n):
        rows = pl.ds(n * rows_half, rows_half)
        return pltpu.make_async_remote_copy(
            src_ref=tables.at[0, rows],
            dst_ref=tables.at[k, rows],
            send_sem=push_send.at[k, n],
            recv_sem=push_recv.at[k, n],
            device_id=column_mate(k),
            device_id_type=MESH,
        )

    def ask(q):
        return pltpu.make_async_remote_copy(
            src_ref=ask_out.at[q],
            dst_ref=ask_in.at[q],
            send_sem=ask_send.at[q],
            recv_sem=ask_recv.at[q],
            device_id=plane_mate(q),
            device_id_type=MESH,
        )

    def reply(q, half):
        return pltpu.make_async_remote_copy(
            src_ref=reply_out.at[q, half],
            dst_ref=reply_in.at[q, half],
            send_sem=reply_send.at[q, half],
            recv_sem=reply_recv.at[q, half],
            device_id=plane_mate(q),
            device_id_type=MESH,
        )

    for fetch in fetches:
        fetch.wait()
    first_w[...] = jnp.zeros_like(first_w)
    for head in range(2):
        first_w[0:inputs, head * hidden : (head + 1) * hidden] = q_in_ref[:, head, :]
    first_w[0:states, 2 * hidden : 3 * hidden] = v_in_ref[...]
    first_w[inputs : inputs + states, 3 * hidden : 4 * hidden] = v_in_ref[...]
    outs = [q_out_ref[n : n + 1, :].astype(f32) for n in range(2)]
    outs.append(v_out_ref[...].astype(f32).reshape(1, hidden))

    lane = iota((8, 128), 1)
    tiles = columns // 128
    part = rows_dev // CHUNKS
    sums = [[jnp.zeros((8, 128), f32) for _ in range(tiles)] for _ in range(6)]

    def collect(kind, first, column):
        for n in range(column.shape[0] // 8):
            tile, at = divmod(first // 8 + n, 128)
            value = jnp.broadcast_to(column[n * 8 : (n + 1) * 8], (8, 128))
            sums[kind][tile] = jnp.where(lane == at, value, sums[kind][tile])

    load.wait()
    for n in range(CHUNKS):
        block = rows_v[n * part : (n + 1) * part, :]
        for head in range(4):
            own = slice(head * hidden, (head + 1) * hidden)
            h1 = jnp.dot(block, first_w[:, own], preferred_element_type=f32)
            h1_ref[n, :, own] = jnp.maximum(h1, 0.0).astype(bf16)
        for head in range(4):
            own = slice(head * hidden, (head + 1) * hidden)
            second_w = q_mid_ref[head] if head < 2 else v_mid_ref[...]
            h2 = jnp.dot(h1_ref[n, :, own], second_w, preferred_element_type=f32)
            terms = jnp.maximum(h2, 0.0) * outs[min(head, 2)]
            terms = sum(terms[:, m : m + 128] for m in range(0, hidden, 128))
            collect(head, n * part, jnp.sum(terms, axis=1, keepdims=True))
        tail = block[:, width - 128 :].astype(f32)
        ends = inputs + states - (width - 128)
        for m in range(2):
            collect(4 + m, n * part, tail[:, ends + m : ends + m + 1])

    for tile in range(tiles):
        q_first, q_second, value_now, value_next, reward, discount = [
            kind[tile] for kind in sums
        ]
        targets = reward + discount * value_next
        q_loss = (q_first - targets) ** 2 + (q_second - targets) ** 2
        gap = jnp.minimum(q_first, q_second) - value_now
        value_loss = jnp.where(gap < 0.0, 0.3, 0.7) * gap * gap
        kinds = (q_first, q_second, value_now, value_next, targets, q_loss, value_loss)
        for kind, value in enumerate(kinds + (jnp.zeros_like(q_loss),)):
            draft[tile, pl.ds(kind, 8, stride=8), :] = value
        tables[0, :, tile * 128 : (tile + 1) * 128] = draft[tile].astype(bf16)

    def begin():
        ready()
        if express:

            @pl.when(source)
            def _():
                for n in parts:
                    far_push(n).start()

        for k in column_mates:
            for n in parts:
                push(k, n).start()

    begin()

    relative = owner_ref[...] ^ me
    plane = relative // mp_size
    row = row_ref[...]
    span = 256
    named = jnp.where(iota((owners, batch), 0) == relative, 1.0, 0.0)
    before = jnp.where(iota((span, span), 0) < iota((span, span), 1), 1.0, 0.0).astype(bf16)
    counts = jnp.dot(
        jnp.concatenate([named[:, n : n + span] for n in range(0, batch, span)], axis=0).astype(bf16),
        before,
        preferred_element_type=f32,
    )
    offset = jnp.zeros((owners, 1), f32)
    ranks = []
    for n in range(batch // span):
        mine = named[:, n * span : (n + 1) * span]
        count = counts[n * owners : (n + 1) * owners]
        ranks.append(jnp.sum(mine * (count + offset), axis=0, keepdims=True))
        offset = offset + count[:, span - 1 : span] + mine[:, span - 1 : span]
    rank = jnp.concatenate(ranks, axis=1).astype(i32)
    place = rank + (plane & 1) * slots
    hot[...] = jnp.where(iota((2 * slots, batch), 0) == place, 1.0, 0.0).astype(bf16)
    group = (plane // 2) * mp_size + (relative & (mp_size - 1))
    listed = iota((pairs, batch), 0) == group
    wanted = jnp.concatenate(
        [
            jnp.where(listed, (row // 8).astype(f32), 0.0),
            jnp.where(listed, (row & 7).astype(f32), 0.0),
        ],
        axis=0,
    ).astype(bf16)
    found = lax.dot_general(
        wanted, hot[...], (((1,), (1,)), ((), ())), preferred_element_type=f32
    )
    asked = (found[:pairs] * 8.0 + found[pairs:]).astype(i32)
    for q in range(dp_size):
        ask_out[q] = asked[
            (q // 2) * mp_size : (q // 2 + 1) * mp_size, (q % 2) * slots : (q % 2 + 1) * slots
        ]
    ask_in[0] = ask_out[0]
    for q in plane_mates:
        ask(q).start()
    if express:
        pl.when(early)(sibling_ask().start)

    where = jnp.broadcast_to(group, (8, batch))
    acc = jnp.zeros((8, batch), f32)

    def pick_of(code):
        return jnp.where(iota((columns, code.shape[1]), 0) == code // 8, 1.0, 0.0).astype(bf16)

    def chosen(found, code):
        low = jnp.broadcast_to(code & 7, (8, code.shape[1]))
        value = found[0:8]
        for n in range(1, 8):
            value = jnp.where(low == n, found[n * 8 : (n + 1) * 8], value)
        return value

    def served(q):
        return (mp == 0) & (dp // 2 == q // 2)

    def gather(acc, half):
        source = jnp.concatenate(
            [
                jnp.concatenate([reply_in[q, half], reply_in[q + 1, half]], axis=1)
                for q in range(0, dp_size, 2)
            ],
            axis=0,
        )
        found = jnp.dot(source, hot[...], preferred_element_type=f32)
        for n in range(dp_size):
            match = where == (n // 2) * mp_size + 2 * half + n % 2
            acc = jnp.where(match, found[n * 8 : (n + 1) * 8], acc)
        return acc

    for q in reversed(plane_mates):
        ask(q).wait_recv()
    if owners <= UNROLL:
        codes = [
            jnp.concatenate([ask_in[q, k : k + 1, :] for q in range(dp_size)], axis=1)
            for k in range(mp_size)
        ]
        for k in range(mp_size):
            picks[k] = pick_of(codes[k])
        for half in range(halves):
            values = []
            for k in (2 * half, 2 * half + 1):
                if k:
                    for n in parts:
                        push(k, n).wait_recv()
                found = jnp.dot(tables[k], picks[k], preferred_element_type=f32)
                values.append(chosen(found, codes[k]))
            both = jnp.concatenate(values, axis=0).astype(bf16)
            for q in (*plane_mates, 0):
                target = reply_out if q else reply_in
                target[q, half] = both[:, q * slots : (q + 1) * slots]
                if q >= 2 and half == halves - 1:
                    pl.when(jnp.logical_not(served(q)))(reply(q, half).start)
                elif q:
                    reply(q, half).start()
        for k in column_mates:
            for n in parts:
                push(k, n).wait_send()
        for q in plane_mates:
            ask(q).wait_send()

        @pl.when(early)
        def _():
            sibling_ask().wait()
            values = {}
            for q, n in away:
                for m in parts:
                    far_pushed(q, n, m).wait_recv()
                code = jnp.concatenate(
                    [
                        ask_out[q, last + n : last + n + 1, :],
                        sibling_asks[q + 1, last + n : last + n + 1, :],
                    ],
                    axis=1,
                )
                found = jnp.dot(
                    far_tables[q // 2 - 1, n], pick_of(code), preferred_element_type=f32
                )
                values[q, n] = chosen(found, code)
                if n:
                    both = jnp.concatenate([values[q, 0], values[q, 1]], axis=0).astype(bf16)
                    reply_in[q, halves - 1] = both[:, :slots]
                    far_out[q // 2 - 1] = both[:, slots:]
                    far_reply(q).start()

        for half in range(halves):
            if half == halves - 1:
                for q in plane_mates:
                    for n in range(halves - 1):
                        reply(q, n).wait_send()
                    if q >= 2:
                        pl.when(jnp.logical_not(served(q)))(reply(q, half).wait_send)
                    else:
                        reply(q, half).wait_send()

                @pl.when(source)
                def _():
                    for n in parts:
                        far_push(n).wait_send()

            near = 2 if half == halves - 1 else dp_size
            for q in range(1, near):
                reply(q, half).wait_recv()
            if near < dp_size:

                @pl.when(jnp.logical_not(early))
                def _():
                    for q in range(near, dp_size):
                        reply(q, half).wait_recv()

                @pl.when(early)
                def _():
                    for q in range(2, dp_size, 2):
                        far_reply(q).wait()

            acc = gather(acc, half)
    else:
        for k in column_mates:
            for n in parts:
                push(k, n).wait()
        for q in plane_mates:
            ask(q).wait_send()

        def answer(n, carry):
            q, half = n // halves, n % halves
            values = []
            for m in range(2):
                code = ask_in[q, pl.ds(2 * half + m, 1), :]
                found = jnp.dot(tables[2 * half + m], pick_of(code), preferred_element_type=f32)
                values.append(chosen(found, code))
            reply_out[q, half] = jnp.concatenate(values, axis=0).astype(bf16)
            return carry

        lax.fori_loop(0, dp_size * halves, answer, 0)
        for half in range(halves):
            reply_in[0, half] = reply_out[0, half]
            for q in plane_mates:
                reply(q, half).start()
        for half in range(halves):
            for q in plane_mates:
                reply(q, half).wait()
        acc = lax.fori_loop(0, halves, lambda n, a: gather(a, n), acc)
    result_ref[...] = acc


def spread(result_ref, q_values_ref, values_ref, targets_ref, q_loss_ref, value_loss_ref):
    q_values_ref[...] = result_ref[0:2]
    values_ref[...] = result_ref[2:4]
    targets_ref[...] = result_ref[4:5]
    q_loss_ref[...] = result_ref[5:6]
    value_loss_ref[...] = result_ref[6:7]


def body(buffer, owner, local_row, q_in, q_mid, q_out, v_in, v_mid, v_out):
    dp_size, mp_size = lax.axis_size("dp"), lax.axis_size("mp")
    owners = dp_size * mp_size
    batch = local_row.shape[0]
    rows_dev, width = buffer.shape
    hidden = v_mid.shape[0]
    most = 4 * batch // owners
    slots = -(-most // 128) * 128
    vmem = pl.BlockSpec(memory_space=pltpu.VMEM)
    hbm = pl.BlockSpec(memory_space=pltpu.HBM)
    dma = pltpu.SemaphoreType.DMA
    result = pl.pallas_call(
        functools.partial(kernel, dp_size, mp_size, slots),
        out_shape=pltpu.VMEM((8, batch), f32),
        in_specs=[hbm] * 9,
        out_specs=vmem,
        scratch_shapes=[
            pltpu.VMEM((1, batch), i32),
            pltpu.VMEM((1, batch), i32),
            pltpu.VMEM((q_in.shape[1], 2, hidden), bf16),
            pltpu.VMEM(q_mid.shape, bf16),
            pltpu.VMEM(q_out.shape, bf16),
            pltpu.VMEM(v_in.shape, bf16),
            pltpu.VMEM(v_mid.shape, bf16),
            pltpu.VMEM(v_out.shape, bf16),
            pltpu.VMEM((rows_dev, width), bf16),
            pltpu.VMEM((width, 4 * hidden), bf16),
            pltpu.VMEM((CHUNKS, rows_dev // CHUNKS, 4 * hidden), bf16),
            pltpu.VMEM((rows_dev // 8 // 128, 64, 128), f32),
            pltpu.VMEM((mp_size, 64, rows_dev // 8), bf16),
            pltpu.VMEM((2 * slots, batch), bf16),
            pltpu.VMEM((mp_size, rows_dev // 8, dp_size * slots), bf16)
            if owners <= UNROLL
            else pltpu.VMEM((8, 128), f32),
            pltpu.VMEM((dp_size, mp_size, slots), i32),
            pltpu.VMEM((dp_size, mp_size, slots), i32),
            pltpu.VMEM((dp_size, mp_size // 2, 16, slots), bf16),
            pltpu.VMEM((dp_size, mp_size // 2, 16, slots), bf16),
            pltpu.VMEM((dp_size, mp_size, slots), i32),
            pltpu.VMEM((dp_size // 2 - 1, 2, 64, rows_dev // 8), bf16),
            pltpu.VMEM((dp_size // 2 - 1, 16, slots), bf16),
            dma,
            dma((8,)),
            dma((mp_size, 2)),
            dma((mp_size, 2)),
            dma((dp_size,)),
            dma((dp_size,)),
            dma((dp_size, mp_size // 2)),
            dma((dp_size, mp_size // 2)),
            dma,
            dma,
            dma((2,)),
            dma((dp_size // 2 - 1, 2, 2)),
            dma((dp_size // 2 - 1,)),
            dma((dp_size // 2 - 1,)),
        ],
        compiler_params=pltpu.CompilerParams(
            collective_id=0, has_side_effects=True, vmem_limit_bytes=48 << 20
        ),
        name="critic_exchange",
    )(
        *(
            pltpu.with_memory_space_constraint(x, pltpu.HBM)
            for x in (
                buffer,
                owner.reshape(1, batch),
                local_row.reshape(1, batch),
                jnp.transpose(q_in, (1, 0, 2)),
                q_mid,
                q_out,
                v_in,
                v_mid,
                v_out,
            )
        )
    )
    one = jax.ShapeDtypeStruct((1, batch), f32)
    two = jax.ShapeDtypeStruct((2, batch), f32)
    outs = pl.pallas_call(
        spread,
        out_shape=(two, two, one, one, one),
        in_specs=[vmem],
        out_specs=(vmem,) * 5,
        compiler_params=pltpu.CompilerParams(vmem_limit_bytes=1 << 20),
        name="spread",
    )(result)
    q_values, values, targets, q_loss, value_loss = outs
    return (
        q_values,
        values,
        targets.reshape(batch),
        q_loss.reshape(batch),
        value_loss.reshape(batch),
    )


def solution(mesh):
    rows = P(("dp", "mp"))
    sides = P(None, ("dp", "mp"))
    return jax.shard_map(
        body,
        mesh=mesh,
        in_specs=(P(("dp", "mp"), None), P(("dp", "mp"), None), rows) + (P(),) * 6,
        out_specs=(sides, sides, rows, rows, rows),
        check_vma=False,
    )
```

```python
import functools

import jax
import jax.numpy as jnp
from jax import lax
from jax.experimental import pallas as pl
from jax.experimental.pallas import tpu as pltpu
from jax.sharding import PartitionSpec as P

MESH = pl.DeviceIdType.MESH
CHUNKS = 4
UNROLL = 64
f32, bf16, i32 = jnp.float32, jnp.bfloat16, jnp.int32


def iota(shape, axis):
    return lax.broadcasted_iota(i32, shape, axis)


def kernel(
    dp_size,
    mp_size,
    slots,
    buffer,
    owner_hbm,
    row_hbm,
    q_in_hbm,
    q_mid_hbm,
    q_out_hbm,
    v_in_hbm,
    v_mid_hbm,
    v_out_hbm,
    result_ref,
    owner_ref,
    row_ref,
    q_in_ref,
    q_mid_ref,
    q_out_ref,
    v_in_ref,
    v_mid_ref,
    v_out_ref,
    rows_v,
    first_w,
    h1_ref,
    draft,
    tables,
    hot,
    picks,
    ask_out,
    ask_in,
    reply_out,
    reply_in,
    sibling_asks,
    far_picks,
    far_tables,
    far_out,
    load_sem,
    fetch_sem,
    push_send,
    push_recv,
    ask_send,
    ask_recv,
    reply_send,
    reply_recv,
    sibling_send,
    sibling_recv,
    far_push_send,
    far_push_recv,
    far_send,
    far_recv,
):
    owners = dp_size * mp_size
    pairs = owners // 2
    halves = mp_size // 2
    rows_dev, width = buffer.shape
    hidden = v_mid_ref.shape[0]
    states = v_in_ref.shape[0]
    inputs = q_in_ref.shape[0]
    batch = row_ref.shape[1]
    columns = rows_dev // 8
    dp, mp = lax.axis_index("dp"), lax.axis_index("mp")
    me = dp * mp_size + mp

    load = pltpu.make_async_copy(buffer, rows_v, load_sem)
    fetches = [
        pltpu.make_async_copy(source, target, fetch_sem.at[number])
        for number, (source, target) in enumerate(
            (
                (q_in_hbm, q_in_ref),
                (v_in_hbm, v_in_ref),
                (q_mid_hbm, q_mid_ref),
                (v_mid_hbm, v_mid_ref),
                (q_out_hbm, q_out_ref),
                (v_out_hbm, v_out_ref),
                (owner_hbm, owner_ref),
                (row_hbm, row_ref),
            )
        )
    ]
    fetches[0].start()
    fetches[1].start()
    load.start()
    for fetch in fetches[2:]:
        fetch.start()

    def flip(value, bits):
        for bit in range(bits.bit_length()):
            if (bits >> bit) & 1:
                step = 1 << bit
                value = value + step * (1 - 2 * ((value // step) % 2))
        return value

    def column_mate(k):
        return (dp, flip(mp, k))

    def plane_mate(q):
        return (flip(dp, q), mp)

    column_mates = range(mp_size - 1, 0, -1)
    plane_mates = range(dp_size - 1, 0, -1)
    express = owners <= UNROLL
    last = mp_size - 2
    early = (mp == 0) & (dp // 2 == 0)
    source = (mp >= last) & (dp // 2 > 0)
    away = [(q, n) for n in range(2) for q in range(2, dp_size, 2)]
    barrier = pltpu.get_barrier_semaphore()
    for k in column_mates:
        pl.semaphore_signal(barrier, inc=1, device_id=column_mate(k), device_id_type=MESH)
    for q in plane_mates:
        pl.semaphore_signal(barrier, inc=1, device_id=plane_mate(q), device_id_type=MESH)

    if express:

        @pl.when(early)
        def _():
            for q, n in away:
                pl.semaphore_signal(
                    barrier, inc=1, device_id=(dp + q, last + n), device_id_type=MESH
                )

    def ready():
        mates = dp_size + mp_size - 2
        if express:
            pl.when(source)(lambda: pl.semaphore_wait(barrier, mates + 1))
            pl.when(jnp.logical_not(source))(lambda: pl.semaphore_wait(barrier, mates))
        else:
            pl.semaphore_wait(barrier, mates)

    tiles = columns // 128
    parts = range(tiles)

    def far_push(n):
        there = (dp // 2 - 1, mp - last, n)
        return pltpu.make_async_remote_copy(
            src_ref=tables.at[0, n],
            dst_ref=far_tables.at[there],
            send_sem=far_push_send.at[n],
            recv_sem=far_push_recv.at[there],
            device_id=(dp % 2, 0),
            device_id_type=MESH,
        )

    def far_pushed(q, n, m):
        return pltpu.make_async_remote_copy(
            src_ref=tables.at[0, m],
            dst_ref=far_tables.at[q // 2 - 1, n, m],
            send_sem=far_push_send.at[m],
            recv_sem=far_push_recv.at[q // 2 - 1, n, m],
            device_id=(dp + q, last + n),
            device_id_type=MESH,
        )

    def sibling_ask():
        return pltpu.make_async_remote_copy(
            src_ref=ask_out,
            dst_ref=sibling_asks,
            send_sem=sibling_send,
            recv_sem=sibling_recv,
            device_id=plane_mate(1),
            device_id_type=MESH,
        )

    def far_reply(q):
        return pltpu.make_async_remote_copy(
            src_ref=far_out.at[q // 2 - 1],
            dst_ref=reply_in.at[q + 1, halves - 1],
            send_sem=far_send.at[q // 2 - 1],
            recv_sem=far_recv.at[q // 2 - 1],
            device_id=plane_mate(1),
            device_id_type=MESH,
        )

    def push(k, n):
        return pltpu.make_async_remote_copy(
            src_ref=tables.at[0, n],
            dst_ref=tables.at[k, n],
            send_sem=push_send.at[k, n],
            recv_sem=push_recv.at[k, n],
            device_id=column_mate(k),
            device_id_type=MESH,
        )

    def ask(q):
        return pltpu.make_async_remote_copy(
            src_ref=ask_out.at[q],
            dst_ref=ask_in.at[q],
            send_sem=ask_send.at[q],
            recv_sem=ask_recv.at[q],
            device_id=plane_mate(q),
            device_id_type=MESH,
        )

    def reply(q, half):
        return pltpu.make_async_remote_copy(
            src_ref=reply_out.at[q, half],
            dst_ref=reply_in.at[q, half],
            send_sem=reply_send.at[q, half],
            recv_sem=reply_recv.at[q, half],
            device_id=plane_mate(q),
            device_id_type=MESH,
        )

    for fetch in fetches:
        fetch.wait()
    first_w[...] = jnp.zeros_like(first_w)
    for head in range(2):
        first_w[0:inputs, head * hidden : (head + 1) * hidden] = q_in_ref[:, head, :]
    first_w[0:states, 2 * hidden : 3 * hidden] = v_in_ref[...]
    first_w[inputs : inputs + states, 3 * hidden : 4 * hidden] = v_in_ref[...]
    outs = [q_out_ref[n : n + 1, :].astype(f32) for n in range(2)]
    outs.append(v_out_ref[...].astype(f32).reshape(1, hidden))

    lane = iota((8, 128), 1)
    part = rows_dev // CHUNKS
    sums = [[jnp.zeros((8, 128), f32) for _ in range(tiles)] for _ in range(6)]

    def collect(kind, first, column):
        for n in range(column.shape[0] // 8):
            tile, at = divmod(first // 8 + n, 128)
            value = jnp.broadcast_to(column[n * 8 : (n + 1) * 8], (8, 128))
            sums[kind][tile] = jnp.where(lane == at, value, sums[kind][tile])

    def begin(n):
        if express:
            pl.when(source)(far_push(n).start)
        for k in column_mates:
            push(k, n).start()

    load.wait()
    for tile in range(tiles):
        for n in range(tile * CHUNKS // tiles, (tile + 1) * CHUNKS // tiles):
            block = rows_v[n * part : (n + 1) * part, :]
            for head in range(4):
                own = slice(head * hidden, (head + 1) * hidden)
                h1 = jnp.dot(block, first_w[:, own], preferred_element_type=f32)
                h1_ref[n, :, own] = jnp.maximum(h1, 0.0).astype(bf16)
            for head in range(4):
                own = slice(head * hidden, (head + 1) * hidden)
                second_w = q_mid_ref[head] if head < 2 else v_mid_ref[...]
                h2 = jnp.dot(h1_ref[n, :, own], second_w, preferred_element_type=f32)
                terms = jnp.maximum(h2, 0.0) * outs[min(head, 2)]
                terms = sum(terms[:, m : m + 128] for m in range(0, hidden, 128))
                collect(head, n * part, jnp.sum(terms, axis=1, keepdims=True))
            tail = block[:, width - 128 :].astype(f32)
            ends = inputs + states - (width - 128)
            for m in range(2):
                collect(4 + m, n * part, tail[:, ends + m : ends + m + 1])
        q_first, q_second, value_now, value_next, reward, discount = [
            kind[tile] for kind in sums
        ]
        targets = reward + discount * value_next
        q_loss = (q_first - targets) ** 2 + (q_second - targets) ** 2
        gap = jnp.minimum(q_first, q_second) - value_now
        value_loss = jnp.where(gap < 0.0, 0.3, 0.7) * gap * gap
        kinds = (q_first, q_second, value_now, value_next, targets, q_loss, value_loss)
        for kind, value in enumerate(kinds + (jnp.zeros_like(q_loss),)):
            draft[tile, pl.ds(kind, 8, stride=8), :] = value
        tables[0, tile] = draft[tile].astype(bf16)
        if tile == 0:
            ready()
        begin(tile)

    relative = owner_ref[...] ^ me
    plane = relative // mp_size
    row = row_ref[...]
    span = 256
    named = jnp.where(iota((owners, batch), 0) == relative, 1.0, 0.0)
    before = jnp.where(iota((span, span), 0) < iota((span, span), 1), 1.0, 0.0).astype(bf16)
    counts = jnp.dot(
        jnp.concatenate([named[:, n : n + span] for n in range(0, batch, span)], axis=0).astype(bf16),
        before,
        preferred_element_type=f32,
    )
    offset = jnp.zeros((owners, 1), f32)
    ranks = []
    for n in range(batch // span):
        mine = named[:, n * span : (n + 1) * span]
        count = counts[n * owners : (n + 1) * owners]
        ranks.append(jnp.sum(mine * (count + offset), axis=0, keepdims=True))
        offset = offset + count[:, span - 1 : span] + mine[:, span - 1 : span]
    rank = jnp.concatenate(ranks, axis=1).astype(i32)
    place = rank + (plane & 1) * slots
    hot[...] = jnp.where(iota((2 * slots, batch), 0) == place, 1.0, 0.0).astype(bf16)
    group = (plane // 2) * mp_size + (relative & (mp_size - 1))
    listed = iota((pairs, batch), 0) == group
    wanted = jnp.concatenate(
        [
            jnp.where(listed, (row // 8).astype(f32), 0.0),
            jnp.where(listed, (row & 7).astype(f32), 0.0),
        ],
        axis=0,
    ).astype(bf16)
    found = lax.dot_general(
        wanted, hot[...], (((1,), (1,)), ((), ())), preferred_element_type=f32
    )
    asked = (found[:pairs] * 8.0 + found[pairs:]).astype(i32)
    for q in range(dp_size):
        ask_out[q] = asked[
            (q // 2) * mp_size : (q // 2 + 1) * mp_size, (q % 2) * slots : (q % 2 + 1) * slots
        ]
    ask_in[0] = ask_out[0]
    for q in plane_mates:
        ask(q).start()
    if express:
        pl.when(early)(sibling_ask().start)

    where = jnp.broadcast_to(group, (8, batch))
    acc = jnp.zeros((8, batch), f32)

    def wide(table):
        return jnp.concatenate([table[n] for n in parts], axis=1)

    def pick_of(code):
        return jnp.where(iota((columns, code.shape[1]), 0) == code // 8, 1.0, 0.0).astype(bf16)

    def chosen(found, code):
        low = jnp.broadcast_to(code & 7, (8, code.shape[1]))
        value = found[0:8]
        for n in range(1, 8):
            value = jnp.where(low == n, found[n * 8 : (n + 1) * 8], value)
        return value

    def far_code(q, n):
        row = slice(last + n, last + n + 1)
        return jnp.concatenate([ask_out[q, row, :], sibling_asks[q + 1, row, :]], axis=1)

    def served(q):
        return (mp == 0) & (dp // 2 == q // 2)

    def gather(acc, half):
        source = jnp.concatenate(
            [
                jnp.concatenate([reply_in[q, half], reply_in[q + 1, half]], axis=1)
                for q in range(0, dp_size, 2)
            ],
            axis=0,
        )
        found = jnp.dot(source, hot[...], preferred_element_type=f32)
        for n in range(dp_size):
            match = where == (n // 2) * mp_size + 2 * half + n % 2
            acc = jnp.where(match, found[n * 8 : (n + 1) * 8], acc)
        return acc

    for q in reversed(plane_mates):
        ask(q).wait_recv()
    if owners <= UNROLL:
        codes = [
            jnp.concatenate([ask_in[q, k : k + 1, :] for q in range(dp_size)], axis=1)
            for k in range(mp_size)
        ]
        for k in range(mp_size):
            picks[k] = pick_of(codes[k])

        @pl.when(early)
        def _():
            sibling_ask().wait()
            for q, n in away:
                far_picks[q // 2 - 1, n] = pick_of(far_code(q, n))

        for half in range(halves):
            values = []
            for k in (2 * half, 2 * half + 1):
                if k:
                    for n in parts:
                        push(k, n).wait_recv()
                found = jnp.dot(wide(tables.at[k]), picks[k], preferred_element_type=f32)
                values.append(chosen(found, codes[k]))
            both = jnp.concatenate(values, axis=0).astype(bf16)
            for q in (*plane_mates, 0):
                target = reply_out if q else reply_in
                target[q, half] = both[:, q * slots : (q + 1) * slots]
                if q >= 2 and half == halves - 1:
                    pl.when(jnp.logical_not(served(q)))(reply(q, half).start)
                elif q:
                    reply(q, half).start()
        for k in column_mates:
            for n in parts:
                push(k, n).wait_send()
        for q in plane_mates:
            ask(q).wait_send()

        @pl.when(early)
        def _():
            values = {}
            for q, n in away:
                for m in parts:
                    far_pushed(q, n, m).wait_recv()
                found = jnp.dot(
                    wide(far_tables.at[q // 2 - 1, n]),
                    far_picks[q // 2 - 1, n],
                    preferred_element_type=f32,
                )
                values[q, n] = chosen(found, far_code(q, n))
                if n:
                    both = jnp.concatenate([values[q, 0], values[q, 1]], axis=0).astype(bf16)
                    reply_in[q, halves - 1] = both[:, :slots]
                    far_out[q // 2 - 1] = both[:, slots:]
                    far_reply(q).start()

        for half in range(halves):
            if half == halves - 1:
                for q in plane_mates:
                    for n in range(halves - 1):
                        reply(q, n).wait_send()
                    if q >= 2:
                        pl.when(jnp.logical_not(served(q)))(reply(q, half).wait_send)
                    else:
                        reply(q, half).wait_send()

                @pl.when(source)
                def _():
                    for n in parts:
                        far_push(n).wait_send()

            near = 2 if half == halves - 1 else dp_size
            for q in range(1, near):
                reply(q, half).wait_recv()
            if near < dp_size:

                @pl.when(jnp.logical_not(early))
                def _():
                    for q in range(near, dp_size):
                        reply(q, half).wait_recv()

                @pl.when(early)
                def _():
                    for q in range(2, dp_size, 2):
                        far_reply(q).wait()

            acc = gather(acc, half)
    else:
        for k in column_mates:
            for n in parts:
                push(k, n).wait()
        for q in plane_mates:
            ask(q).wait_send()

        def answer(n, carry):
            q, half = n // halves, n % halves
            values = []
            for m in range(2):
                code = ask_in[q, pl.ds(2 * half + m, 1), :]
                found = jnp.dot(wide(tables.at[2 * half + m]), pick_of(code), preferred_element_type=f32)
                values.append(chosen(found, code))
            reply_out[q, half] = jnp.concatenate(values, axis=0).astype(bf16)
            return carry

        lax.fori_loop(0, dp_size * halves, answer, 0)
        for half in range(halves):
            reply_in[0, half] = reply_out[0, half]
            for q in plane_mates:
                reply(q, half).start()
        for half in range(halves):
            for q in plane_mates:
                reply(q, half).wait()
        acc = lax.fori_loop(0, halves, lambda n, a: gather(a, n), acc)
    result_ref[...] = acc


def spread(result_ref, q_values_ref, values_ref, targets_ref, q_loss_ref, value_loss_ref):
    q_values_ref[...] = result_ref[0:2]
    values_ref[...] = result_ref[2:4]
    targets_ref[...] = result_ref[4:5]
    q_loss_ref[...] = result_ref[5:6]
    value_loss_ref[...] = result_ref[6:7]


def body(buffer, owner, local_row, q_in, q_mid, q_out, v_in, v_mid, v_out):
    dp_size, mp_size = lax.axis_size("dp"), lax.axis_size("mp")
    owners = dp_size * mp_size
    batch = local_row.shape[0]
    rows_dev, width = buffer.shape
    hidden = v_mid.shape[0]
    most = 4 * batch // owners
    slots = -(-most // 128) * 128
    vmem = pl.BlockSpec(memory_space=pltpu.VMEM)
    hbm = pl.BlockSpec(memory_space=pltpu.HBM)
    dma = pltpu.SemaphoreType.DMA
    result = pl.pallas_call(
        functools.partial(kernel, dp_size, mp_size, slots),
        out_shape=pltpu.VMEM((8, batch), f32),
        in_specs=[hbm] * 9,
        out_specs=vmem,
        scratch_shapes=[
            pltpu.VMEM((1, batch), i32),
            pltpu.VMEM((1, batch), i32),
            pltpu.VMEM((q_in.shape[1], 2, hidden), bf16),
            pltpu.VMEM(q_mid.shape, bf16),
            pltpu.VMEM(q_out.shape, bf16),
            pltpu.VMEM(v_in.shape, bf16),
            pltpu.VMEM(v_mid.shape, bf16),
            pltpu.VMEM(v_out.shape, bf16),
            pltpu.VMEM((rows_dev, width), bf16),
            pltpu.VMEM((width, 4 * hidden), bf16),
            pltpu.VMEM((CHUNKS, rows_dev // CHUNKS, 4 * hidden), bf16),
            pltpu.VMEM((rows_dev // 8 // 128, 64, 128), f32),
            pltpu.VMEM((mp_size, rows_dev // 8 // 128, 64, 128), bf16),
            pltpu.VMEM((2 * slots, batch), bf16),
            pltpu.VMEM((mp_size, rows_dev // 8, dp_size * slots), bf16)
            if owners <= UNROLL
            else pltpu.VMEM((8, 128), f32),
            pltpu.VMEM((dp_size, mp_size, slots), i32),
            pltpu.VMEM((dp_size, mp_size, slots), i32),
            pltpu.VMEM((dp_size, mp_size // 2, 16, slots), bf16),
            pltpu.VMEM((dp_size, mp_size // 2, 16, slots), bf16),
            pltpu.VMEM((dp_size, mp_size, slots), i32),
            pltpu.VMEM((dp_size // 2 - 1, 2, rows_dev // 8, 2 * slots), bf16)
            if owners <= UNROLL
            else pltpu.VMEM((8, 128), f32),
            pltpu.VMEM((dp_size // 2 - 1, 2, rows_dev // 8 // 128, 64, 128), bf16),
            pltpu.VMEM((dp_size // 2 - 1, 16, slots), bf16),
            dma,
            dma((8,)),
            dma((mp_size, 2)),
            dma((mp_size, 2)),
            dma((dp_size,)),
            dma((dp_size,)),
            dma((dp_size, mp_size // 2)),
            dma((dp_size, mp_size // 2)),
            dma,
            dma,
            dma((2,)),
            dma((dp_size // 2 - 1, 2, 2)),
            dma((dp_size // 2 - 1,)),
            dma((dp_size // 2 - 1,)),
        ],
        compiler_params=pltpu.CompilerParams(
            collective_id=0, has_side_effects=True, vmem_limit_bytes=48 << 20
        ),
        name="critic_exchange",
    )(
        *(
            pltpu.with_memory_space_constraint(x, pltpu.HBM)
            for x in (
                buffer,
                owner.reshape(1, batch),
                local_row.reshape(1, batch),
                jnp.transpose(q_in, (1, 0, 2)),
                q_mid,
                q_out,
                v_in,
                v_mid,
                v_out,
            )
        )
    )
    one = jax.ShapeDtypeStruct((1, batch), f32)
    two = jax.ShapeDtypeStruct((2, batch), f32)
    outs = pl.pallas_call(
        spread,
        out_shape=(two, two, one, one, one),
        in_specs=[vmem],
        out_specs=(vmem,) * 5,
        compiler_params=pltpu.CompilerParams(vmem_limit_bytes=1 << 20),
        name="spread",
    )(result)
    q_values, values, targets, q_loss, value_loss = outs
    return (
        q_values,
        values,
        targets.reshape(batch),
        q_loss.reshape(batch),
        value_loss.reshape(batch),
    )


def solution(mesh):
    rows = P(("dp", "mp"))
    sides = P(None, ("dp", "mp"))
    return jax.shard_map(
        body,
        mesh=mesh,
        in_specs=(P(("dp", "mp"), None), P(("dp", "mp"), None), rows) + (P(),) * 6,
        out_specs=(sides, sides, rows, rows, rows),
        check_vma=False,
    )
```

```python
import functools

import jax
import jax.numpy as jnp
from jax import lax
from jax.experimental import pallas as pl
from jax.experimental.pallas import tpu as pltpu
from jax.sharding import PartitionSpec as P

MESH = pl.DeviceIdType.MESH
CHUNKS = 4
UNROLL = 64
f32, bf16, i32 = jnp.float32, jnp.bfloat16, jnp.int32


def iota(shape, axis):
    return lax.broadcasted_iota(i32, shape, axis)


def kernel(
    dp_size,
    mp_size,
    slots,
    buffer,
    owner_hbm,
    row_hbm,
    q_in_hbm,
    q_mid_hbm,
    q_out_hbm,
    v_in_hbm,
    v_mid_hbm,
    v_out_hbm,
    result_ref,
    owner_ref,
    row_ref,
    q_in_ref,
    q_mid_ref,
    q_out_ref,
    v_in_ref,
    v_mid_ref,
    v_out_ref,
    rows_v,
    first_w,
    h1_ref,
    draft,
    tables,
    hot,
    picks,
    ask_out,
    ask_in,
    reply_out,
    reply_in,
    sibling_asks,
    far_picks,
    far_tables,
    far_out,
    load_sem,
    fetch_sem,
    push_send,
    push_recv,
    ask_send,
    ask_recv,
    reply_send,
    reply_recv,
    sibling_send,
    sibling_recv,
    far_push_send,
    far_push_recv,
    far_send,
    far_recv,
):
    owners = dp_size * mp_size
    pairs = owners // 2
    halves = mp_size // 2
    rows_dev, width = buffer.shape
    hidden = v_mid_ref.shape[0]
    states = v_in_ref.shape[0]
    inputs = q_in_ref.shape[0]
    batch = row_ref.shape[1]
    columns = rows_dev // 8
    dp, mp = lax.axis_index("dp"), lax.axis_index("mp")
    me = dp * mp_size + mp

    load = pltpu.make_async_copy(buffer, rows_v, load_sem)
    fetches = [
        pltpu.make_async_copy(source, target, fetch_sem.at[number])
        for number, (source, target) in enumerate(
            (
                (q_in_hbm, q_in_ref),
                (v_in_hbm, v_in_ref),
                (q_mid_hbm, q_mid_ref),
                (v_mid_hbm, v_mid_ref),
                (q_out_hbm, q_out_ref),
                (v_out_hbm, v_out_ref),
                (owner_hbm, owner_ref),
                (row_hbm, row_ref),
            )
        )
    ]
    fetches[0].start()
    fetches[1].start()
    load.start()
    for fetch in fetches[2:]:
        fetch.start()

    def flip(value, bits):
        for bit in range(bits.bit_length()):
            if (bits >> bit) & 1:
                step = 1 << bit
                value = value + step * (1 - 2 * ((value // step) % 2))
        return value

    def column_mate(k):
        return (dp, flip(mp, k))

    def plane_mate(q):
        return (flip(dp, q), mp)

    column_mates = range(mp_size - 1, 0, -1)
    plane_mates = range(dp_size - 1, 0, -1)
    express = owners <= UNROLL
    last = mp_size - 2
    early = (mp == 0) & (dp // 2 == 0)
    source = (mp >= last) & (dp // 2 > 0)
    away = [(q, n) for n in range(2) for q in range(2, dp_size, 2)]
    barrier = pltpu.get_barrier_semaphore()
    for k in column_mates:
        pl.semaphore_signal(barrier, inc=1, device_id=column_mate(k), device_id_type=MESH)
    for q in plane_mates:
        pl.semaphore_signal(barrier, inc=1, device_id=plane_mate(q), device_id_type=MESH)

    if express:

        @pl.when(early)
        def _():
            for q, n in away:
                pl.semaphore_signal(
                    barrier, inc=1, device_id=(dp + q, last + n), device_id_type=MESH
                )

    def ready():
        mates = dp_size + mp_size - 2
        if express:
            pl.when(source)(lambda: pl.semaphore_wait(barrier, mates + 1))
            pl.when(jnp.logical_not(source))(lambda: pl.semaphore_wait(barrier, mates))
        else:
            pl.semaphore_wait(barrier, mates)

    tiles = columns // 128
    parts = range(tiles)

    def far_push(n):
        there = (dp // 2 - 1, mp - last, n)
        return pltpu.make_async_remote_copy(
            src_ref=tables.at[0, n],
            dst_ref=far_tables.at[there],
            send_sem=far_push_send.at[n],
            recv_sem=far_push_recv.at[there],
            device_id=(dp % 2, 0),
            device_id_type=MESH,
        )

    def far_pushed(q, n, m):
        return pltpu.make_async_remote_copy(
            src_ref=tables.at[0, m],
            dst_ref=far_tables.at[q // 2 - 1, n, m],
            send_sem=far_push_send.at[m],
            recv_sem=far_push_recv.at[q // 2 - 1, n, m],
            device_id=(dp + q, last + n),
            device_id_type=MESH,
        )

    def sibling_ask():
        return pltpu.make_async_remote_copy(
            src_ref=ask_out,
            dst_ref=sibling_asks,
            send_sem=sibling_send,
            recv_sem=sibling_recv,
            device_id=plane_mate(1),
            device_id_type=MESH,
        )

    def far_reply(q):
        return pltpu.make_async_remote_copy(
            src_ref=far_out.at[q // 2 - 1],
            dst_ref=reply_in.at[q + 1, halves - 1],
            send_sem=far_send.at[q // 2 - 1],
            recv_sem=far_recv.at[q // 2 - 1],
            device_id=plane_mate(1),
            device_id_type=MESH,
        )

    def push(k, n):
        return pltpu.make_async_remote_copy(
            src_ref=tables.at[0, n],
            dst_ref=tables.at[k, n],
            send_sem=push_send.at[k, n],
            recv_sem=push_recv.at[k, n],
            device_id=column_mate(k),
            device_id_type=MESH,
        )

    def ask(q):
        return pltpu.make_async_remote_copy(
            src_ref=ask_out.at[q],
            dst_ref=ask_in.at[q],
            send_sem=ask_send.at[q],
            recv_sem=ask_recv.at[q],
            device_id=plane_mate(q),
            device_id_type=MESH,
        )

    def reply(q, half):
        return pltpu.make_async_remote_copy(
            src_ref=reply_out.at[q, half],
            dst_ref=reply_in.at[q, half],
            send_sem=reply_send.at[q, half],
            recv_sem=reply_recv.at[q, half],
            device_id=plane_mate(q),
            device_id_type=MESH,
        )

    for fetch in fetches:
        fetch.wait()
    first_w[...] = jnp.zeros_like(first_w)
    for head in range(2):
        first_w[0:inputs, head * hidden : (head + 1) * hidden] = q_in_ref[:, head, :]
    first_w[0:states, 2 * hidden : 3 * hidden] = v_in_ref[...]
    first_w[inputs : inputs + states, 3 * hidden : 4 * hidden] = v_in_ref[...]
    outs = [q_out_ref[n : n + 1, :].astype(f32) for n in range(2)]
    outs.append(v_out_ref[...].astype(f32).reshape(1, hidden))

    lane = iota((8, 128), 1)
    part = rows_dev // CHUNKS
    sums = [[jnp.zeros((8, 128), f32) for _ in range(tiles)] for _ in range(6)]

    def collect(kind, first, column):
        for n in range(column.shape[0] // 8):
            tile, at = divmod(first // 8 + n, 128)
            value = jnp.broadcast_to(column[n * 8 : (n + 1) * 8], (8, 128))
            sums[kind][tile] = jnp.where(lane == at, value, sums[kind][tile])

    def begin(n):
        if express:
            pl.when(source)(far_push(n).start)
        for k in column_mates:
            push(k, n).start()

    def group_of(relative):
        return (relative // (2 * mp_size)) * mp_size + (relative & (mp_size - 1))

    def prepare():
        relative = owner_ref[...] ^ me
        plane = relative // mp_size
        row = row_ref[...]
        span = 256
        named = jnp.where(iota((owners, batch), 0) == relative, 1.0, 0.0)
        before = jnp.where(iota((span, span), 0) < iota((span, span), 1), 1.0, 0.0).astype(bf16)
        counts = jnp.dot(
            jnp.concatenate([named[:, n : n + span] for n in range(0, batch, span)], axis=0).astype(bf16),
            before,
            preferred_element_type=f32,
        )
        offset = jnp.zeros((owners, 1), f32)
        ranks = []
        for n in range(batch // span):
            mine = named[:, n * span : (n + 1) * span]
            count = counts[n * owners : (n + 1) * owners]
            ranks.append(jnp.sum(mine * (count + offset), axis=0, keepdims=True))
            offset = offset + count[:, span - 1 : span] + mine[:, span - 1 : span]
        rank = jnp.concatenate(ranks, axis=1).astype(i32)
        place = rank + (plane & 1) * slots
        hot[...] = jnp.where(iota((2 * slots, batch), 0) == place, 1.0, 0.0).astype(bf16)
        group = group_of(relative)
        listed = iota((pairs, batch), 0) == group
        wanted = jnp.concatenate(
            [
                jnp.where(listed, (row // 8).astype(f32), 0.0),
                jnp.where(listed, (row & 7).astype(f32), 0.0),
            ],
            axis=0,
        ).astype(bf16)
        found = lax.dot_general(
            wanted, hot[...], (((1,), (1,)), ((), ())), preferred_element_type=f32
        )
        asked = (found[:pairs] * 8.0 + found[pairs:]).astype(i32)
        for q in range(dp_size):
            ask_out[q] = asked[
                (q // 2) * mp_size : (q // 2 + 1) * mp_size, (q % 2) * slots : (q % 2 + 1) * slots
            ]
        ask_in[0] = ask_out[0]

    def send_asks():
        for q in plane_mates:
            ask(q).start()
        if express:
            pl.when(early)(sibling_ask().start)

    inner = mp < halves
    load.wait()
    for tile in range(tiles):
        for n in range(tile * CHUNKS // tiles, (tile + 1) * CHUNKS // tiles):
            block = rows_v[n * part : (n + 1) * part, :]
            for head in range(4):
                own = slice(head * hidden, (head + 1) * hidden)
                h1 = jnp.dot(block, first_w[:, own], preferred_element_type=f32)
                h1_ref[n, :, own] = jnp.maximum(h1, 0.0).astype(bf16)
            for head in range(4):
                own = slice(head * hidden, (head + 1) * hidden)
                second_w = q_mid_ref[head] if head < 2 else v_mid_ref[...]
                h2 = jnp.dot(h1_ref[n, :, own], second_w, preferred_element_type=f32)
                terms = jnp.maximum(h2, 0.0) * outs[min(head, 2)]
                terms = sum(terms[:, m : m + 128] for m in range(0, hidden, 128))
                collect(head, n * part, jnp.sum(terms, axis=1, keepdims=True))
            tail = block[:, width - 128 :].astype(f32)
            ends = inputs + states - (width - 128)
            for m in range(2):
                collect(4 + m, n * part, tail[:, ends + m : ends + m + 1])
        q_first, q_second, value_now, value_next, reward, discount = [
            kind[tile] for kind in sums
        ]
        targets = reward + discount * value_next
        q_loss = (q_first - targets) ** 2 + (q_second - targets) ** 2
        gap = jnp.minimum(q_first, q_second) - value_now
        value_loss = jnp.where(gap < 0.0, 0.3, 0.7) * gap * gap
        kinds = (q_first, q_second, value_now, value_next, targets, q_loss, value_loss)
        for kind, value in enumerate(kinds + (jnp.zeros_like(q_loss),)):
            draft[tile, pl.ds(kind, 8, stride=8), :] = value
        tables[0, tile] = draft[tile].astype(bf16)
        if tile == 0:
            pl.when(inner)(prepare)
            ready()
        begin(tile)
        if tile == 0:
            pl.when(inner)(send_asks)

    @pl.when(jnp.logical_not(inner))
    def _():
        prepare()
        send_asks()

    relative = owner_ref[...] ^ me
    group = group_of(relative)
    where = jnp.broadcast_to(group, (8, batch))
    acc = jnp.zeros((8, batch), f32)

    def wide(table):
        return jnp.concatenate([table[n] for n in parts], axis=1)

    def pick_of(code):
        return jnp.where(iota((columns, code.shape[1]), 0) == code // 8, 1.0, 0.0).astype(bf16)

    def chosen(found, code):
        low = jnp.broadcast_to(code & 7, (8, code.shape[1]))
        value = found[0:8]
        for n in range(1, 8):
            value = jnp.where(low == n, found[n * 8 : (n + 1) * 8], value)
        return value

    def far_code(q, n):
        row = slice(last + n, last + n + 1)
        return jnp.concatenate([ask_out[q, row, :], sibling_asks[q + 1, row, :]], axis=1)

    def served(q):
        return (mp == 0) & (dp // 2 == q // 2)

    def gather(acc, half):
        source = jnp.concatenate(
            [
                jnp.concatenate([reply_in[q, half], reply_in[q + 1, half]], axis=1)
                for q in range(0, dp_size, 2)
            ],
            axis=0,
        )
        found = jnp.dot(source, hot[...], preferred_element_type=f32)
        for n in range(dp_size):
            match = where == (n // 2) * mp_size + 2 * half + n % 2
            acc = jnp.where(match, found[n * 8 : (n + 1) * 8], acc)
        return acc

    for q in reversed(plane_mates):
        ask(q).wait_recv()
    if owners <= UNROLL:
        codes = [
            jnp.concatenate([ask_in[q, k : k + 1, :] for q in range(dp_size)], axis=1)
            for k in range(mp_size)
        ]
        for k in range(mp_size):
            picks[k] = pick_of(codes[k])

        @pl.when(early)
        def _():
            sibling_ask().wait()
            for q, n in away:
                far_picks[q // 2 - 1, n] = pick_of(far_code(q, n))

        for half in range(halves):
            values = []
            for k in (2 * half, 2 * half + 1):
                if k:
                    for n in parts:
                        push(k, n).wait_recv()
                found = jnp.dot(wide(tables.at[k]), picks[k], preferred_element_type=f32)
                values.append(chosen(found, codes[k]))
            both = jnp.concatenate(values, axis=0).astype(bf16)
            for q in (*plane_mates, 0):
                target = reply_out if q else reply_in
                target[q, half] = both[:, q * slots : (q + 1) * slots]
                if q >= 2 and half == halves - 1:
                    pl.when(jnp.logical_not(served(q)))(reply(q, half).start)
                elif q:
                    reply(q, half).start()
        for k in column_mates:
            for n in parts:
                push(k, n).wait_send()
        for q in plane_mates:
            ask(q).wait_send()

        @pl.when(early)
        def _():
            values = {}
            for q, n in away:
                for m in parts:
                    far_pushed(q, n, m).wait_recv()
                found = jnp.dot(
                    wide(far_tables.at[q // 2 - 1, n]),
                    far_picks[q // 2 - 1, n],
                    preferred_element_type=f32,
                )
                values[q, n] = chosen(found, far_code(q, n))
                if n:
                    both = jnp.concatenate([values[q, 0], values[q, 1]], axis=0).astype(bf16)
                    reply_in[q, halves - 1] = both[:, :slots]
                    far_out[q // 2 - 1] = both[:, slots:]
                    far_reply(q).start()

        for half in range(halves):
            if half == halves - 1:
                for q in plane_mates:
                    for n in range(halves - 1):
                        reply(q, n).wait_send()
                    if q >= 2:
                        pl.when(jnp.logical_not(served(q)))(reply(q, half).wait_send)
                    else:
                        reply(q, half).wait_send()

                @pl.when(source)
                def _():
                    for n in parts:
                        far_push(n).wait_send()

            near = 2 if half == halves - 1 else dp_size
            for q in range(1, near):
                reply(q, half).wait_recv()
            if near < dp_size:

                @pl.when(jnp.logical_not(early))
                def _():
                    for q in range(near, dp_size):
                        reply(q, half).wait_recv()

                @pl.when(early)
                def _():
                    for q in range(2, dp_size, 2):
                        far_reply(q).wait()

            acc = gather(acc, half)
    else:
        for k in column_mates:
            for n in parts:
                push(k, n).wait()
        for q in plane_mates:
            ask(q).wait_send()

        def answer(n, carry):
            q, half = n // halves, n % halves
            values = []
            for m in range(2):
                code = ask_in[q, pl.ds(2 * half + m, 1), :]
                found = jnp.dot(wide(tables.at[2 * half + m]), pick_of(code), preferred_element_type=f32)
                values.append(chosen(found, code))
            reply_out[q, half] = jnp.concatenate(values, axis=0).astype(bf16)
            return carry

        lax.fori_loop(0, dp_size * halves, answer, 0)
        for half in range(halves):
            reply_in[0, half] = reply_out[0, half]
            for q in plane_mates:
                reply(q, half).start()
        for half in range(halves):
            for q in plane_mates:
                reply(q, half).wait()
        acc = lax.fori_loop(0, halves, lambda n, a: gather(a, n), acc)
    result_ref[...] = acc


def spread(result_ref, q_values_ref, values_ref, targets_ref, q_loss_ref, value_loss_ref):
    q_values_ref[...] = result_ref[0:2]
    values_ref[...] = result_ref[2:4]
    targets_ref[...] = result_ref[4:5]
    q_loss_ref[...] = result_ref[5:6]
    value_loss_ref[...] = result_ref[6:7]


def body(buffer, owner, local_row, q_in, q_mid, q_out, v_in, v_mid, v_out):
    dp_size, mp_size = lax.axis_size("dp"), lax.axis_size("mp")
    owners = dp_size * mp_size
    batch = local_row.shape[0]
    rows_dev, width = buffer.shape
    hidden = v_mid.shape[0]
    most = 4 * batch // owners
    slots = -(-most // 128) * 128
    vmem = pl.BlockSpec(memory_space=pltpu.VMEM)
    hbm = pl.BlockSpec(memory_space=pltpu.HBM)
    dma = pltpu.SemaphoreType.DMA
    result = pl.pallas_call(
        functools.partial(kernel, dp_size, mp_size, slots),
        out_shape=pltpu.VMEM((8, batch), f32),
        in_specs=[hbm] * 9,
        out_specs=vmem,
        scratch_shapes=[
            pltpu.VMEM((1, batch), i32),
            pltpu.VMEM((1, batch), i32),
            pltpu.VMEM((q_in.shape[1], 2, hidden), bf16),
            pltpu.VMEM(q_mid.shape, bf16),
            pltpu.VMEM(q_out.shape, bf16),
            pltpu.VMEM(v_in.shape, bf16),
            pltpu.VMEM(v_mid.shape, bf16),
            pltpu.VMEM(v_out.shape, bf16),
            pltpu.VMEM((rows_dev, width), bf16),
            pltpu.VMEM((width, 4 * hidden), bf16),
            pltpu.VMEM((CHUNKS, rows_dev // CHUNKS, 4 * hidden), bf16),
            pltpu.VMEM((rows_dev // 8 // 128, 64, 128), f32),
            pltpu.VMEM((mp_size, rows_dev // 8 // 128, 64, 128), bf16),
            pltpu.VMEM((2 * slots, batch), bf16),
            pltpu.VMEM((mp_size, rows_dev // 8, dp_size * slots), bf16)
            if owners <= UNROLL
            else pltpu.VMEM((8, 128), f32),
            pltpu.VMEM((dp_size, mp_size, slots), i32),
            pltpu.VMEM((dp_size, mp_size, slots), i32),
            pltpu.VMEM((dp_size, mp_size // 2, 16, slots), bf16),
            pltpu.VMEM((dp_size, mp_size // 2, 16, slots), bf16),
            pltpu.VMEM((dp_size, mp_size, slots), i32),
            pltpu.VMEM((dp_size // 2 - 1, 2, rows_dev // 8, 2 * slots), bf16)
            if owners <= UNROLL
            else pltpu.VMEM((8, 128), f32),
            pltpu.VMEM((dp_size // 2 - 1, 2, rows_dev // 8 // 128, 64, 128), bf16),
            pltpu.VMEM((dp_size // 2 - 1, 16, slots), bf16),
            dma,
            dma((8,)),
            dma((mp_size, 2)),
            dma((mp_size, 2)),
            dma((dp_size,)),
            dma((dp_size,)),
            dma((dp_size, mp_size // 2)),
            dma((dp_size, mp_size // 2)),
            dma,
            dma,
            dma((2,)),
            dma((dp_size // 2 - 1, 2, 2)),
            dma((dp_size // 2 - 1,)),
            dma((dp_size // 2 - 1,)),
        ],
        compiler_params=pltpu.CompilerParams(
            collective_id=0, has_side_effects=True, vmem_limit_bytes=48 << 20
        ),
        name="critic_exchange",
    )(
        *(
            pltpu.with_memory_space_constraint(x, pltpu.HBM)
            for x in (
                buffer,
                owner.reshape(1, batch),
                local_row.reshape(1, batch),
                jnp.transpose(q_in, (1, 0, 2)),
                q_mid,
                q_out,
                v_in,
                v_mid,
                v_out,
            )
        )
    )
    one = jax.ShapeDtypeStruct((1, batch), f32)
    two = jax.ShapeDtypeStruct((2, batch), f32)
    outs = pl.pallas_call(
        spread,
        out_shape=(two, two, one, one, one),
        in_specs=[vmem],
        out_specs=(vmem,) * 5,
        compiler_params=pltpu.CompilerParams(vmem_limit_bytes=1 << 20),
        name="spread",
    )(result)
    q_values, values, targets, q_loss, value_loss = outs
    return (
        q_values,
        values,
        targets.reshape(batch),
        q_loss.reshape(batch),
        value_loss.reshape(batch),
    )


def solution(mesh):
    rows = P(("dp", "mp"))
    sides = P(None, ("dp", "mp"))
    return jax.shard_map(
        body,
        mesh=mesh,
        in_specs=(P(("dp", "mp"), None), P(("dp", "mp"), None), rows) + (P(),) * 6,
        out_specs=(sides, sides, rows, rows, rows),
        check_vma=False,
    )
```
